32 devices in a mesh: section: 2 (over x), patch: 4 (over z), fsdp: 4 (over y, core).
Axes of the slice: x: 2, y: 2, z: 4, core: 2. Of those that a mesh axis runs over, the one named last changes fastest.
Arguments:
- latent: float32 [8, 4, 256, 64], P('fsdp', 'patch', 'section'), may hold values from -60 to 60
- counts: int32 [8, 4], P('fsdp'), may hold values from 64 to 256, as said below
- steps_idx: int32 [8], P('fsdp'), may hold values from 0 to 49
- embed_weight: bfloat16 [64, 1536], replicated, may hold values from -0.75 to 0.75
- wqkv: bfloat16 [2, 1536, 4608], P('section', 'fsdp'), may hold values from -0.15625 to 0.15625
- wo: bfloat16 [2, 1536, 1536], P('section', 'fsdp'), may hold values from -0.15625 to 0.15625
- qk_gain: float32 [2, 3072], P('section'), may hold values from 0.1 to 1.9
- modulation: float32 [2, 50, 4608], P('section'), may hold values from -3 to 3
- head_mod: float32 [50, 3072], replicated, may hold values from -3 to 3
- head_weight: bfloat16 [1536, 64], replicated, may hold values from -0.15625 to 0.15625
- stale_cache: bfloat16 [2, 8, 4, 256, 3072], P('section', 'fsdp', 'patch'), may hold values from -210 to 210
Outputs:
- velocity: float32 [8, 4, 256, 64], P('fsdp', 'patch', 'section')
- new_latent: float32 [8, 4, 256, 64], P('fsdp', 'patch', 'section')
- cache_out: bfloat16 [2, 8, 4, 256, 3072], P('section', 'fsdp', 'patch')
The draws below stay inside these ranges and needn't reach their ends.
Inputs may be any that keep to these rules, and one draw needn't show every extreme that they name: `counts`: in every video one patch holds exactly 256 tokens.
All inputs are finite; a program needn't handle non-finite values.
Results may differ from the reference program's by a relative error of at most 0.0071.
Values may be sent and summed in bfloat16 or wider, within the bound.
A program may use at most 192 MiB of HBM per device.

```python
import math
import jax
import jax.numpy as jnp
from jax import lax

D = 1536
HEADS = 12
HD = 128
CH = 64
P_SIZE = 256
TSTEPS = 50
LAYERS = 2
VIDEOS = 8
N_PATCH = 4


def draw_latent(key, part):
    array_shape = (VIDEOS, N_PATCH, P_SIZE, CH)
    key_base = jax.random.fold_in(key, 0)
    normal_draw = jax.random.normal(key_base, array_shape, jnp.float32)
    return jnp.clip(normal_draw, -4.0, 4.0)


def draw_counts(key, part):
    key_count, key_full = jax.random.split(key)
    drawn_counts = jax.random.randint(key_count, (VIDEOS, N_PATCH), P_SIZE // 4, P_SIZE + 1)
    full_patch = jax.random.randint(key_full, (VIDEOS,), 0, N_PATCH)
    return jnp.where(jnp.arange(N_PATCH)[None, :] == full_patch[:, None], P_SIZE, drawn_counts).astype(jnp.int32)


def draw_stale_cache(key, part):
    array_shape = (LAYERS, VIDEOS, N_PATCH, P_SIZE, 2 * D)
    key_base = jax.random.fold_in(key, 0)
    base_draw = jnp.clip(jax.random.normal(key_base, array_shape, jnp.float32), -4.0, 4.0)
    return base_draw.astype(jnp.bfloat16)


def touch_ends(values, key, low, largest):
    longest = values.shape.index(max(values.shape))
    spots = []
    for shift in (0, 1):
        where = [jax.random.randint(jax.random.fold_in(key, axis), (), 0, length) for axis, length in enumerate(values.shape)]
        where[longest] = (where[longest] + shift) % values.shape[longest]
        spots.append(tuple(where))
    return values.at[spots[0]].set(low).at[spots[1]].set(largest)


def level_of(own_key, dims, pieces, least, high):
    def one(position, blocks):
        heights = jax.random.uniform(jax.random.fold_in(jax.random.fold_in(own_key, 6), position), (blocks,), jnp.float32, least / len(pieces), high / len(pieces))
        return jnp.repeat(jnp.exp(heights), dims[position] // blocks).reshape((-1,) + (1,) * (len(dims) - position - 1))

    loudness = one(*pieces[0])
    for cut in pieces[1:]:
        loudness = loudness * one(*cut)
    return loudness


def noise(stream_key, extent, width, reach, cuts=(), kind=jnp.bfloat16):
    level = level_of(stream_key, extent, cuts, -0.22, 0.18) if cuts else 1.0
    drawn = jax.random.normal(stream_key, extent, jnp.float32) * width * level
    return jnp.minimum(jnp.maximum(drawn, -reach), reach).astype(kind)


def setup_inputs(seed: int = 0) -> dict:
    key_list = jax.random.split(jax.random.key(seed), 12)
    return {
        "latent": draw_latent(jax.random.fold_in(key_list[11], 71), 0),
        "counts": draw_counts(jax.random.fold_in(key_list[11], 71), 0),
        "steps_idx": touch_ends(jax.random.randint(key_list[2], (VIDEOS,), 0, TSTEPS), jax.random.fold_in(key_list[2], 1), 0, TSTEPS - 1).astype(jnp.int32),
        "embed_weight": noise(key_list[3], (CH, D), CH ** -0.5, 0.75),
        "wqkv": noise(key_list[4], (LAYERS, D, 3 * D), D ** -0.5, 0.15625, ((0, 2), (1, 4))),
        "wo": noise(key_list[5], (LAYERS, D, D), D ** -0.5, 0.15625, ((0, 2), (1, 4))),
        "qk_gain": jnp.clip(1.0 + 0.18 * jax.random.normal(key_list[6], (LAYERS, 2 * D), jnp.float32), 0.1, 1.9),
        "modulation": noise(key_list[7], (LAYERS, TSTEPS, 3 * D), 0.5, 3.0, ((0, 2),), jnp.float32),
        "head_mod": noise(key_list[8], (TSTEPS, 2 * D), 0.5, 3.0, (), jnp.float32),
        "head_weight": noise(key_list[9], (D, CH), D ** -0.5, 0.15625),
        "stale_cache": draw_stale_cache(jax.random.fold_in(key_list[11], 71), 0),
    }


EPS = 1e-06

def layer_norm(hidden):
    center = hidden - lax.optimization_barrier(jnp.mean(hidden, axis=-1, keepdims=True))
    return center * lax.rsqrt(lax.optimization_barrier(jnp.mean(center * center, axis=-1, keepdims=True)) + EPS)

def rms_norm(values_in, gain_vec):
    return values_in * lax.rsqrt(lax.optimization_barrier(jnp.mean(values_in * values_in, axis=-1, keepdims=True)) + EPS) * gain_vec

def sigma_of(step_float):
    remain = 1.0 - step_float / TSTEPS
    return 5.0 * remain / (1.0 + 4.0 * remain)

def attend(queries, key_rows, value_rows, key_live):
    query_heads = queries.reshape(queries.shape[0], HEADS, HD).astype(jnp.float32)
    key_heads = key_rows.reshape(key_rows.shape[0], HEADS, HD).astype(jnp.float32)
    value_heads = value_rows.reshape(value_rows.shape[0], HEADS, HD).astype(jnp.float32)
    scores = jnp.einsum('qhd,khd->hqk', query_heads, key_heads) / math.sqrt(HD)
    scores = jnp.where(key_live[None, None, :], scores, -jnp.inf)
    top_score = lax.optimization_barrier(jnp.max(scores, axis=-1, keepdims=True))
    exp_scores = jnp.exp(scores - top_score)
    denom_sum = lax.optimization_barrier(jnp.sum(exp_scores, axis=-1))
    weights = lax.optimization_barrier(exp_scores.astype(jnp.bfloat16)).astype(jnp.float32)
    mixed_out = jnp.einsum('hqk,khd->qhd', weights, value_heads) / jnp.transpose(denom_sum)[:, :, None]
    return mixed_out.reshape(queries.shape[0], HEADS * HD).astype(jnp.bfloat16)

def reference(latent, counts, steps_idx, embed_weight, wqkv, wo, qk_gain, modulation, head_mod, head_weight, stale_cache):

    def video_step(inputs):
        latent_v, counts_v, step_v, stale_v = inputs
        live = jnp.arange(P_SIZE)[None, :] < counts_v[:, None]
        hidden = jnp.dot(latent_v.astype(jnp.bfloat16).reshape(-1, CH), embed_weight, preferred_element_type=jnp.float32)
        caches = []
        for layer_index in range(LAYERS):
            mod_row = modulation[layer_index, step_v]
            shift_vec, scale_vec, gate_vec = (mod_row[:D], mod_row[D:2 * D], mod_row[2 * D:])
            normed = (layer_norm(hidden) * (1.0 + scale_vec) + shift_vec).astype(jnp.bfloat16)
            projected = jnp.dot(normed, wqkv[layer_index], preferred_element_type=jnp.float32)
            queries = rms_norm(projected[:, :D], qk_gain[layer_index, :D]).astype(jnp.bfloat16)
            fresh_keys = rms_norm(projected[:, D:2 * D], qk_gain[layer_index, D:]).astype(jnp.bfloat16)
            fresh_values = projected[:, 2 * D:].astype(jnp.bfloat16)
            fresh_kv = jnp.concatenate([fresh_keys, fresh_values], axis=-1).reshape(N_PATCH, P_SIZE, 2 * D)
            caches.append(jnp.where(live[:, :, None], fresh_kv, jnp.zeros_like(fresh_kv)))
            query_blocks = queries.reshape(N_PATCH, P_SIZE, D)
            outputs = []
            for patch_slot in range(N_PATCH):
                seen_rows = stale_v[layer_index].at[patch_slot].set(fresh_kv[patch_slot]).reshape(N_PATCH * P_SIZE, 2 * D)
                outputs.append(attend(query_blocks[patch_slot], seen_rows[:, :D], seen_rows[:, D:], live.reshape(-1)))
            attended = jnp.concatenate(outputs, axis=0)
            hidden = hidden + gate_vec * jnp.dot(attended, wo[layer_index], preferred_element_type=jnp.float32)
            if layer_index + 1 < LAYERS:
                hidden = lax.optimization_barrier(hidden.astype(jnp.bfloat16)).astype(jnp.float32)
        head_row = head_mod[step_v]
        head_in = (layer_norm(hidden) * (1.0 + head_row[D:]) + head_row[:D]).astype(jnp.bfloat16)
        velocity = jnp.dot(head_in, head_weight, preferred_element_type=jnp.float32).reshape(N_PATCH, P_SIZE, CH)
        velocity = jnp.where(live[:, :, None], velocity, jnp.zeros_like(velocity))
        step_float = step_v.astype(jnp.float32)
        step_delta = sigma_of(step_float + 1.0) - sigma_of(step_float)
        return (velocity, latent_v + step_delta * velocity, jnp.stack(caches))
    velocity, new_latent, cache_all = lax.map(video_step, (latent, counts, steps_idx, jnp.moveaxis(stale_cache, 1, 0)))
    return (velocity, new_latent, jnp.moveaxis(cache_all, 0, 1))
```

```python
import functools
import math

import jax
import jax.numpy as jnp
from jax import lax
from jax.experimental import pallas as pl
from jax.experimental.pallas import tpu as pltpu
from jax.sharding import PartitionSpec as P

HEADS = 12
HD = 128
TSTEPS = 50
EPS = 1e-06
MESH = pl.DeviceIdType.MESH
TILE = 512
META_ROWS = 16


def sigma_of(step_float):
    remain = 1.0 - step_float / TSTEPS
    return 5.0 * remain / (1.0 + 4.0 * remain)


def remote(src, dst, send_sem, recv_sem, target):
    return pltpu.make_async_remote_copy(
        src_ref=src,
        dst_ref=dst,
        send_sem=send_sem,
        recv_sem=recv_sem,
        device_id=target,
        device_id_type=MESH,
    )


def step_kernel(
    chips,
    latent,
    counts,
    steps,
    embed,
    gain,
    modulation,
    head_mod,
    head_weight,
    wqkv,
    wo,
    stale,
    velocity,
    fresh,
    wbuf,
    kvbuf,
    live_buf,
    meta,
    lat_stage,
    lat_owner,
    lat_home,
    hid,
    proj,
    normed,
    q_buf,
    k_buf,
    v_buf,
    attended,
    h1_stage,
    h1_buf,
    h1_home,
    fresh_stage,
    vel_stage,
    vel_buf,
    w_local,
    wy_send,
    wy_recv,
    ws_send,
    ws_recv,
    wf_send,
    wf_recv,
    kv_send,
    kv_recv,
    kf_send,
    kf_recv,
    meta_send,
    meta_recv,
    lo_send,
    lo_recv,
    lh_send,
    lh_recv,
    h1_send,
    h1_recv,
    hh_send,
    hh_recv,
    vel_send,
    vel_recv,
    out_sem,
):
    s = lax.axis_index("section")
    z = lax.axis_index("patch")
    f = lax.axis_index("fsdp")
    c = lax.rem(f, 2)
    g = f // 2
    model = embed.shape[1]
    shard_rows = wqkv.shape[1]
    slots = kvbuf.shape[2]
    half = slots // 2
    patches = kvbuf.shape[1]

    def device(section, patch, chip, core):
        return {"section": section, "patch": patch, "fsdp": 2 * chip + core}

    sibling = device(s, z, g, 1 - c)
    across = z // 2
    spot = lax.rem(z, 2)

    barrier = pltpu.get_barrier_semaphore()
    greeted = 0
    for ds in range(2):
        for dz in range(patches):
            for dc in range(2):
                if ds or dz or dc:
                    pl.semaphore_signal(
                        barrier,
                        inc=1,
                        device_id=device(
                            lax.rem(s + ds, 2), lax.rem(z + dz, patches), g, lax.rem(c + dc, 2)
                        ),
                        device_id_type=MESH,
                    )
                    greeted += 1
    for dg in range(1, chips):
        pl.semaphore_signal(
            barrier, inc=1, device_id=device(s, z, lax.rem(g + dg, chips), c), device_id_type=MESH
        )
        greeted += 1
    pl.semaphore_wait(barrier, greeted)

    def weight_src(t):
        if t < 3:
            return wqkv.at[0, :, t * model : (t + 1) * model]
        return wo.at[0]

    def weight_rows(t, owner):
        return wbuf.at[t, pl.ds(pl.multiple_of(owner * shard_rows, shard_rows), shard_rows), :]

    def w_own(t):
        return pltpu.make_async_copy(weight_src(t), weight_rows(t, f), w_local.at[t])

    def w_across(t, dg):
        return remote(
            weight_src(t),
            weight_rows(t, f),
            wy_send.at[t, dg],
            wy_recv.at[t, dg],
            device(s, z, lax.rem(g + dg, chips), c),
        )

    def w_sibling(t):
        return remote(weight_src(t), weight_rows(t, f), ws_send.at[t], ws_recv.at[t], sibling)

    def w_forward(t, dg):
        rows = weight_rows(t, 2 * lax.rem(g + chips - dg, chips) + c)
        return remote(rows, rows, wf_send.at[t, dg], wf_recv.at[t, dg], sibling)

    def kv_src(j, x):
        return stale.at[0, j, 0, :, x * model : (x + 1) * model]

    def kv_is_self(j, x):
        return jnp.logical_and(2 * c + j == z, c == x)

    def kv_remote(j, x):
        return remote(
            kv_src(j, x),
            kvbuf.at[x, z],
            kv_send.at[j, x],
            kv_recv.at[z],
            device(s, 2 * c + j, g, x),
        )

    def kv_arrival(p):
        return remote(kvbuf.at[c, p], kvbuf.at[c, p], kf_send.at[p], kv_recv.at[p], sibling)

    def kv_forward(p):
        return remote(kvbuf.at[c, p], kvbuf.at[c, p], kf_send.at[p], kf_recv.at[p], sibling)

    for t in range(4):
        for dg in range(1, chips):
            w_across(t, dg).start()
        if t == 0:
            for j in range(2):
                for x in range(2):

                    @pl.when(kv_is_self(j, x))
                    def _():
                        pltpu.make_async_copy(kv_src(j, x), kvbuf.at[x, z], kv_recv.at[z]).start()

                    @pl.when(jnp.logical_not(kv_is_self(j, x)))
                    def _():
                        kv_remote(j, x).start()

    for j in range(2):
        step = steps[j]
        video = 2 * c + j
        for part in range(3):
            meta[video, part : part + 1, :] = modulation[
                0, pl.ds(step, 1), part * model : (part + 1) * model
            ]
        for part in range(2):
            meta[video, 3 + part : 4 + part, :] = head_mod[
                pl.ds(step, 1), part * model : (part + 1) * model
            ]
        for p in range(patches):
            meta[video, 5 + p : 6 + p, :] = jnp.full((1, model), counts[j, p].astype(jnp.float32))
        lat_stage[j] = latent[j, 0].astype(jnp.bfloat16)
    mine = meta.at[pl.ds(2 * c, 2)]
    meta_copy = remote(mine, mine, meta_send, meta_recv, sibling)
    meta_copy.start()

    def lat_owner_self(j):
        return jnp.logical_and(s == 0, jnp.logical_and(2 * c + j == z, across == c))

    def lat_owner_copy(j):
        return remote(
            lat_stage.at[j],
            lat_owner.at[spot, pl.ds(pl.multiple_of(s * half, half), half)],
            lo_send.at[j],
            lo_recv.at[spot, s],
            device(0, 2 * c + j, g, across),
        )

    def lat_home_copy(j):
        return remote(
            lat_stage.at[j],
            lat_home.at[j, pl.ds(pl.multiple_of(s * half, half), half)],
            lh_send.at[j],
            lh_recv.at[j, s],
            device(0, z, g, c),
        )

    for j in range(2):

        @pl.when(lat_owner_self(j))
        def _():
            pltpu.make_async_copy(
                lat_stage.at[j],
                lat_owner.at[spot, pl.ds(pl.multiple_of(s * half, half), half)],
                lo_recv.at[spot, s],
            ).start()

        @pl.when(jnp.logical_not(lat_owner_self(j)))
        def _():
            lat_owner_copy(j).start()

        @pl.when(s == 1)
        def _():
            lat_home_copy(j).start()

        @pl.when(s == 0)
        def _():
            pltpu.make_async_copy(
                lat_stage.at[j], lat_home.at[j, :half], lh_recv.at[j, 0]
            ).start()

    for t in range(4):
        w_own(t).start()
        w_sibling(t).start()

    meta_copy.wait()

    for p in range(patches):
        row = lax.broadcasted_iota(jnp.int32, (slots, HD), 0).astype(jnp.float32)
        live = row < meta[z, 5 + p : 6 + p, :HD]
        live_buf[p] = jnp.where(live, 1.0, 0.0).astype(jnp.bfloat16)

    def weights_arrive(t):
        for dg in range(1, chips):
            w_across(t, dg).wait_recv()
            w_forward(t, dg).start()
        w_own(t).wait()
        w_sibling(t).wait_recv()
        for dg in range(1, chips):
            w_forward(t, dg).wait_recv()

    def mask_rows(p, key_ref, value_ref):
        first = key_ref[0:16, :][0:1, :]
        last_row = meta[z, pl.ds(5 + p, 1), :]

        def rows_of(i, carry):
            rows = pl.ds(pl.multiple_of(i * 16, 16), 16)
            row = lax.broadcasted_iota(jnp.int32, (16, model), 0) + i * 16
            live = row.astype(jnp.float32) < last_row
            key_ref[rows, :] = jnp.where(
                live, key_ref[rows, :].astype(jnp.float32), first.astype(jnp.float32)
            ).astype(jnp.bfloat16)
            value_ref[rows, :] = jnp.where(
                live, value_ref[rows, :].astype(jnp.float32), 0.0
            ).astype(jnp.bfloat16)
            return carry

        lax.fori_loop(0, slots // 16, rows_of, 0)

    def caches_arrive():
        for p in range(patches):
            kv_arrival(p).wait_recv()
            kv_forward(p).start()
        for p in range(patches):
            kv_forward(p).wait()
            mask_rows(p, kvbuf.at[0, p], kvbuf.at[1, p])

    def multiply(left, weight, sink):
        def tile(i, carry):
            cols = pl.ds(pl.multiple_of(i * TILE, TILE), TILE)
            sink(
                cols, jnp.dot(left[...], weight[:, cols], preferred_element_type=jnp.float32)
            )
            return carry

        lax.fori_loop(0, model // TILE, tile, 0)

    def sink_proj(cols, product):
        proj[:, cols] = product

    def sink_hid(cols, product):
        hid[:, cols] = product

    def center_rows(rows):
        values = hid[rows, :]
        center = values - jnp.mean(values, axis=-1, keepdims=True)
        return center * lax.rsqrt(jnp.mean(center * center, axis=-1, keepdims=True) + EPS)

    def norm_rows(video, shift_row, scale_row):
        shift = meta[video, shift_row : shift_row + 1, :]
        scale = 1.0 + meta[video, scale_row : scale_row + 1, :]

        def rows_of(i, carry):
            rows = pl.ds(pl.multiple_of(i * 16, 16), 16)
            normed[rows, :] = (center_rows(rows) * scale + shift).astype(jnp.bfloat16)
            return carry

        lax.fori_loop(0, slots // 16, rows_of, 0)

    def rms_rows(out_ref, out_cols, gain_cols, factor):
        gains = gain[:, gain_cols] * factor

        def rows_of(i, carry):
            rows = pl.ds(pl.multiple_of(i * 16, 16), 16)
            values = proj[rows, :]
            scaled = values * lax.rsqrt(jnp.mean(values * values, axis=-1, keepdims=True) + EPS)
            out_ref[rows, out_cols] = (scaled * gains).astype(jnp.bfloat16)
            return carry

        lax.fori_loop(0, slots // 16, rows_of, 0)

    def attend(k):
        own = 2 * c + k

        def head(h, carry):
            cols = pl.ds(pl.multiple_of(h * HD, HD), HD)
            query = q_buf[:, cols]
            scores = []
            for b in range(patches):
                p = lax.rem(own + b, patches)
                keys = k_buf[:, cols] if b == 0 else kvbuf[0, p, :, cols]
                scores.append(
                    lax.dot_general(
                        query, keys, (((1,), (1,)), ((), ())), preferred_element_type=jnp.float32
                    )
                )
            top = scores[0]
            for score in scores[1:]:
                top = jnp.maximum(top, score)
            top = jnp.max(top, axis=1, keepdims=True)
            mixed = None
            for b in range(patches):
                p = lax.rem(own + b, patches)
                weight = jnp.exp2(scores[b] - top).astype(jnp.bfloat16)
                values = v_buf[:, cols] if b == 0 else kvbuf[1, p, :, cols]
                both = jnp.concatenate([values, live_buf[p]], axis=1)
                part = jnp.dot(weight, both, preferred_element_type=jnp.float32)
                mixed = part if mixed is None else mixed + part
            attended[:, cols] = (mixed[:, :HD] / mixed[:, HD:]).astype(jnp.bfloat16)
            return carry

        lax.fori_loop(0, HEADS, head, 0)

    def home_of(k, section):
        return device(section, 2 * c + k, g, across)

    def home_is_self(k):
        return jnp.logical_and(2 * c + k == z, across == c)

    def h1_over(k):
        return remote(h1_stage.at[k], h1_buf.at[k], h1_send.at[k], h1_recv.at[k], device(1, z, g, c))

    def h1_to_home(k):
        return remote(
            h1_buf.at[k], h1_home.at[spot], hh_send.at[k], hh_recv.at[spot], home_of(k, 1)
        )

    def vel_src(k, section):
        return vel_stage.at[k, section * half : (section + 1) * half]

    def vel_to_home(k, section):
        return remote(
            vel_src(k, section),
            vel_buf.at[spot],
            vel_send.at[k, section],
            vel_recv.at[spot],
            home_of(k, section),
        )

    @pl.when(s == 1)
    def _():
        for t in range(4):
            weights_arrive(t)
        caches_arrive()

    factor = math.log2(math.e) / math.sqrt(HD)

    def block(k, carry):
        early = jnp.logical_and(s == 0, k == 0)

        @pl.when(s == 0)
        def _():
            for part in range(2):
                rows = pl.ds(part * half, half)
                remote(
                    lat_owner.at[k, rows],
                    lat_owner.at[k, rows],
                    lo_send.at[0],
                    lo_recv.at[k, part],
                    sibling,
                ).wait_recv()
            multiply(lat_owner.at[k], embed, sink_hid)

        @pl.when(s == 1)
        def _():
            h1_over(k).wait_recv()

            @pl.when(home_is_self(k))
            def _():
                pltpu.make_async_copy(h1_buf.at[k], h1_home.at[spot], hh_recv.at[spot]).start()

            @pl.when(jnp.logical_not(home_is_self(k)))
            def _():
                h1_to_home(k).start()

            hid[...] = h1_buf[k].astype(jnp.float32)

        norm_rows(z, 0, 1)

        @pl.when(early)
        def _():
            weights_arrive(0)

        multiply(normed, wbuf.at[0], sink_proj)
        rms_rows(q_buf, slice(None), slice(0, model), factor)

        @pl.when(early)
        def _():
            weights_arrive(1)

        multiply(normed, wbuf.at[1], sink_proj)
        rms_rows(k_buf, slice(None), slice(model, 2 * model), 1.0)

        @pl.when(early)
        def _():
            weights_arrive(2)

        def sink_value(cols, product):
            v_buf[:, cols] = product.astype(jnp.bfloat16)

        multiply(normed, wbuf.at[2], sink_value)
        mask_rows(2 * c + k, k_buf, v_buf)

        @pl.when(early)
        def _():
            caches_arrive()

        attend(k)

        @pl.when(early)
        def _():
            weights_arrive(3)

        def sink_update(cols, product):
            hid[:, cols] = hid[:, cols] + meta[z, 2:3, cols] * product

        multiply(attended, wbuf.at[3], sink_update)

        @pl.when(s == 0)
        def _():
            h1_stage[k] = hid[...].astype(jnp.bfloat16)
            h1_over(k).start()

        @pl.when(s == 1)
        def _():
            norm_rows(z, 3, 4)
            vel_stage[k] = jnp.dot(
                normed[...], head_weight[...], preferred_element_type=jnp.float32
            )
            for section in range(2):
                if section == 0:
                    vel_to_home(k, section).start()
                else:

                    @pl.when(home_is_self(k))
                    def _():
                        pltpu.make_async_copy(
                            vel_src(k, 1), vel_buf.at[spot], vel_recv.at[spot]
                        ).start()

                    @pl.when(jnp.logical_not(home_is_self(k)))
                    def _():
                        vel_to_home(k, 1).start()

        return carry

    lax.fori_loop(0, 2, block, 0)

    def fresh_out(j):
        return pltpu.make_async_copy(fresh_stage.at[j], fresh.at[0, j, 0], out_sem.at[j])

    def home(j, carry):
        @pl.when(s == 0)
        def _():
            for part in range(2):
                rows = pl.ds(part * half, half)
                remote(
                    lat_home.at[j, rows],
                    lat_home.at[j, rows],
                    lh_send.at[0],
                    lh_recv.at[j, part],
                    sibling,
                ).wait_recv()
            multiply(lat_home.at[j], embed, sink_hid)

        @pl.when(s == 1)
        def _():
            remote(
                h1_home.at[j], h1_home.at[j], hh_send.at[0], hh_recv.at[j], sibling
            ).wait_recv()
            hid[...] = h1_home[j].astype(jnp.float32)

        norm_rows(2 * c + j, 0, 1)
        multiply(normed, wbuf.at[1], sink_proj)
        rms_rows(fresh_stage.at[j], slice(0, model), slice(model, 2 * model), 1.0)

        def sink_fresh(cols, product):
            proj[:, cols] = product

        multiply(normed, wbuf.at[2], sink_fresh)
        fresh_stage[j, :, model:] = proj[...].astype(jnp.bfloat16)
        fresh_out(j).start()
        return carry

    lax.fori_loop(0, 2, home, 0)

    for t in range(4):
        for dg in range(1, chips):
            w_across(t, dg).wait_send()
            w_forward(t, dg).wait_send()
        w_sibling(t).wait_send()
    for j in range(2):
        for x in range(2):

            @pl.when(jnp.logical_not(kv_is_self(j, x)))
            def _():
                kv_remote(j, x).wait_send()

        @pl.when(jnp.logical_not(lat_owner_self(j)))
        def _():
            lat_owner_copy(j).wait_send()

        @pl.when(s == 1)
        def _():
            lat_home_copy(j).wait_send()

    for k in range(2):

        @pl.when(s == 0)
        def _():
            h1_over(k).wait_send()

        @pl.when(s == 1)
        def _():
            vel_to_home(k, 0).wait_send()

            @pl.when(jnp.logical_not(home_is_self(k)))
            def _():
                h1_to_home(k).wait_send()
                vel_to_home(k, 1).wait_send()

    for j in range(2):
        remote(
            vel_buf.at[j], vel_buf.at[j], vel_send.at[0, 0], vel_recv.at[j], sibling
        ).wait_recv()
        velocity[j, 0] = vel_buf[j]
        fresh_out(j).wait()


def body(
    chips,
    latent,
    counts,
    steps_idx,
    embed_weight,
    wqkv,
    wo,
    qk_gain,
    modulation,
    head_mod,
    head_weight,
    stale_cache,
):
    videos, _, half, channels = latent.shape
    patches = counts.shape[1]
    slots = stale_cache.shape[3]
    model = embed_weight.shape[1]
    assert videos == 2 and patches == 4
    bf16, f32 = jnp.bfloat16, jnp.float32
    vmem = pl.BlockSpec(memory_space=pltpu.VMEM)
    smem = pl.BlockSpec(memory_space=pltpu.SMEM)
    anywhere = pl.BlockSpec(memory_space=pl.ANY)
    dma = pltpu.SemaphoreType.DMA
    velocity, fresh = pl.pallas_call(
        functools.partial(step_kernel, chips),
        in_specs=[vmem, smem, smem, vmem, vmem, vmem, vmem, vmem, anywhere, anywhere, anywhere],
        out_specs=[vmem, anywhere],
        out_shape=[
            jax.ShapeDtypeStruct(latent.shape, f32),
            jax.ShapeDtypeStruct(stale_cache.shape, bf16),
        ],
        scratch_shapes=[
            pltpu.VMEM((4, model, model), bf16),
            pltpu.VMEM((2, patches, slots, model), bf16),
            pltpu.VMEM((patches, slots, HD), bf16),
            pltpu.VMEM((4, META_ROWS, model), f32),
            pltpu.VMEM((2, half, channels), bf16),
            pltpu.VMEM((2, slots, channels), bf16),
            pltpu.VMEM((2, slots, channels), bf16),
            pltpu.VMEM((slots, model), f32),
            pltpu.VMEM((slots, model), f32),
            pltpu.VMEM((slots, model), bf16),
            pltpu.VMEM((slots, model), bf16),
            pltpu.VMEM((slots, model), bf16),
            pltpu.VMEM((slots, model), bf16),
            pltpu.VMEM((slots, model), bf16),
            pltpu.VMEM((2, slots, model), bf16),
            pltpu.VMEM((2, slots, model), bf16),
            pltpu.VMEM((2, slots, model), bf16),
            pltpu.VMEM((2, slots, 2 * model), bf16),
            pltpu.VMEM((2, slots, channels), f32),
            pltpu.VMEM((2, half, channels), f32),
            dma((4,)),
            dma((4, chips)),
            dma((4, chips)),
            dma((4,)),
            dma((4,)),
            dma((4, chips)),
            dma((4, chips)),
            dma((2, 2)),
            dma((patches,)),
            dma((patches,)),
            dma((patches,)),
            dma,
            dma,
            dma((2,)),
            dma((2, 2)),
            dma((2,)),
            dma((2, 2)),
            dma((2,)),
            dma((2,)),
            dma((2,)),
            dma((2,)),
            dma((2, 2)),
            dma((2,)),
            dma((2,)),
        ],
        compiler_params=pltpu.CompilerParams(
            collective_id=0, has_side_effects=True, vmem_limit_bytes=58 * 1024 * 1024
        ),
    )(
        latent,
        counts,
        steps_idx,
        embed_weight,
        qk_gain,
        modulation,
        head_mod,
        head_weight,
        wqkv,
        wo,
        stale_cache,
    )
    own = lax.dynamic_index_in_dim(counts, lax.axis_index("patch"), 1)
    live = jnp.arange(slots, dtype=jnp.int32)[None, :] < own
    cache_out = jnp.where(live[None, :, None, :, None], fresh, jnp.zeros_like(fresh))
    mine = jnp.arange(half, dtype=jnp.int32)[None, :] + half * lax.axis_index("section") < own
    velocity = jnp.where(mine[:, None, :, None], velocity, 0.0)
    step_float = steps_idx.astype(f32)
    step_delta = sigma_of(step_float + 1.0) - sigma_of(step_float)
    new_latent = latent + step_delta[:, None, None, None] * velocity
    return velocity, new_latent, cache_out


def solution(mesh):
    chips = mesh.shape["fsdp"] // 2
    in_specs = (
        P("fsdp", "patch", "section", None),
        P("fsdp", None),
        P("fsdp"),
        P(),
        P("section", "fsdp", None),
        P("section", "fsdp", None),
        P("section", None),
        P("section", None, None),
        P(),
        P(),
        P("section", "fsdp", "patch", None, None),
    )
    out_specs = (
        P("fsdp", "patch", "section", None),
        P("fsdp", "patch", "section", None),
        P("section", "fsdp", "patch", None, None),
    )
    return jax.shard_map(
        functools.partial(body, chips),
        mesh=mesh,
        in_specs=in_specs,
        out_specs=out_specs,
        check_vma=False,
    )
```

```python
import functools
import math

import jax
import jax.numpy as jnp
from jax import lax
from jax.experimental import pallas as pl
from jax.experimental.pallas import tpu as pltpu
from jax.sharding import PartitionSpec as P

HEADS = 12
HD = 128
TSTEPS = 50
EPS = 1e-06
MESH = pl.DeviceIdType.MESH
TILE = 512
META_ROWS = 16
SHARED = {1: 0, 3: 1}


def sigma_of(step_float):
    remain = 1.0 - step_float / TSTEPS
    return 5.0 * remain / (1.0 + 4.0 * remain)


def remote(src, dst, send_sem, recv_sem, target):
    return pltpu.make_async_remote_copy(
        src_ref=src,
        dst_ref=dst,
        send_sem=send_sem,
        recv_sem=recv_sem,
        device_id=target,
        device_id_type=MESH,
    )


def step_kernel(
    chips,
    latent,
    counts,
    steps,
    embed,
    gain,
    modulation,
    head_mod,
    head_weight,
    wqkv,
    wo,
    stale,
    velocity,
    new_latent,
    fresh,
    wbuf,
    kvbuf,
    live_buf,
    meta,
    lat_stage,
    lat_owner,
    lat_home,
    hid,
    proj,
    normed,
    q_buf,
    k_buf,
    v_buf,
    attended,
    h1_stage,
    h1_buf,
    h1_home,
    fresh_stage,
    vel_stage,
    vel_buf,
    w_local,
    wy_send,
    wy_recv,
    ws_send,
    ws_recv,
    wf_send,
    wf_recv,
    zr_send,
    zr_recv,
    zf_send,
    zf_recv,
    kv_send,
    kv_recv,
    kf_send,
    kf_recv,
    meta_send,
    meta_recv,
    lo_send,
    lo_recv,
    lh_send,
    lh_recv,
    h1_send,
    h1_recv,
    hh_send,
    hh_recv,
    vel_send,
    vel_recv,
    out_sem,
):
    s = lax.axis_index("section")
    z = lax.axis_index("patch")
    f = lax.axis_index("fsdp")
    c = lax.rem(f, 2)
    g = f // 2
    model = embed.shape[1]
    shard_rows = wqkv.shape[1]
    slots = kvbuf.shape[2]
    half = slots // 2
    part_cols = model // 2
    tiles = model // TILE
    patches = kvbuf.shape[1]

    def device(section, patch, chip, core):
        return {"section": section, "patch": patch, "fsdp": 2 * chip + core}

    sibling = device(s, z, g, 1 - c)
    across = z // 2
    spot = lax.rem(z, 2)

    barrier = pltpu.get_barrier_semaphore()
    greeted = 0
    for ds in range(2):
        for dz in range(patches):
            for dc in range(2):
                if ds or dz or dc:
                    pl.semaphore_signal(
                        barrier,
                        inc=1,
                        device_id=device(
                            lax.rem(s + ds, 2), lax.rem(z + dz, patches), g, lax.rem(c + dc, 2)
                        ),
                        device_id_type=MESH,
                    )
                    greeted += 1
    for dg in range(1, chips):
        pl.semaphore_signal(
            barrier, inc=1, device_id=device(s, z, lax.rem(g + dg, chips), c), device_id_type=MESH
        )
        greeted += 1
    pl.semaphore_wait(barrier, greeted)

    def weight_src(t):
        if t < 3:
            return wqkv.at[0, :, t * model : (t + 1) * model]
        return wo.at[0]

    def weight_rows(t, owner):
        return wbuf.at[t, pl.ds(pl.multiple_of(owner * shard_rows, shard_rows), shard_rows), :]

    def w_own(t):
        return pltpu.make_async_copy(weight_src(t), weight_rows(t, f), w_local.at[t])

    def cols_of(q, start=0):
        return pl.ds(pl.multiple_of(start + q * part_cols, part_cols), part_cols)

    def owner_back(dg):
        return 2 * lax.rem(g + chips - dg, chips) + c

    def w_across(t, dg):
        src, dst = weight_src(t), weight_rows(t, f)
        if t in SHARED:
            src = wo.at[0, :, cols_of(spot)] if t == 3 else wqkv.at[0, :, cols_of(spot, t * model)]
            dst = part_of(t, 0, spot)
        return remote(
            src,
            dst,
            wy_send.at[t, dg],
            wy_recv.at[t, dg],
            device(s, z, lax.rem(g + dg, chips), c),
        )

    def part_of(t, dg, q):
        rows = pl.ds(pl.multiple_of(owner_back(dg) * shard_rows, shard_rows), shard_rows)
        return wbuf.at[t, rows, cols_of(q)]

    def part_forward(t, dg, q):
        part, at = part_of(t, dg, q), SHARED[t]
        return remote(part, part, zf_send.at[at, dg, q], zf_recv.at[at, dg, q], sibling)

    def part_pair(t, dg, q):
        part, at = part_of(t, dg, q), SHARED[t]
        return remote(
            part, part, zr_send.at[at, dg], zr_recv.at[at, dg], device(s, z + 1 - 2 * spot, g, c)
        )

    def parts_first(t):
        for dg in range(1, chips):
            w_across(t, dg).wait_recv()
            part_pair(t, dg, spot).start()
            part_forward(t, dg, spot).start()

    def parts_second(t):
        for dg in range(1, chips):
            part_pair(t, dg, 1 - spot).wait_recv()
            part_forward(t, dg, 1 - spot).start()
        w_own(t).wait()
        w_sibling(t).wait_recv()
        for dg in range(1, chips):
            for q in range(2):
                part_forward(t, dg, q).wait_recv()

    def parts_sent():
        for t in SHARED:
            for dg in range(1, chips):
                part_pair(t, dg, spot).wait_send()
                for q in range(2):
                    part_forward(t, dg, q).wait_send()

    def w_sibling(t):
        return remote(weight_src(t), weight_rows(t, f), ws_send.at[t], ws_recv.at[t], sibling)

    def w_forward(t, dg):
        rows = weight_rows(t, 2 * lax.rem(g + chips - dg, chips) + c)
        return remote(rows, rows, wf_send.at[t, dg], wf_recv.at[t, dg], sibling)

    def kv_src(j, x):
        return stale.at[0, j, 0, :, x * model : (x + 1) * model]

    def kv_is_self(j, x):
        return jnp.logical_and(2 * c + j == z, c == x)

    def kv_remote(j, x):
        return remote(
            kv_src(j, x),
            kvbuf.at[x, z],
            kv_send.at[j, x],
            kv_recv.at[z],
            device(s, 2 * c + j, g, x),
        )

    def kv_arrival(p):
        return remote(kvbuf.at[c, p], kvbuf.at[c, p], kf_send.at[p], kv_recv.at[p], sibling)

    def kv_forward(p):
        return remote(kvbuf.at[c, p], kvbuf.at[c, p], kf_send.at[p], kf_recv.at[p], sibling)

    def kv_start(j, x):
        @pl.when(kv_is_self(j, x))
        def _():
            pltpu.make_async_copy(kv_src(j, x), kvbuf.at[x, z], kv_recv.at[z]).start()

        @pl.when(jnp.logical_not(kv_is_self(j, x)))
        def _():
            kv_remote(j, x).start()

    def across_start(t):
        for dg in range(1, chips):
            w_across(t, dg).start()

    across_start(1)
    across_start(3)
    kv_start(0, 0)
    kv_start(0, 1)

    for j in range(2):
        step = steps[j]
        video = 2 * c + j
        for part in range(3):
            meta[video, part : part + 1, :] = modulation[
                step, :, part * model : (part + 1) * model
            ]
        for part in range(2):
            meta[video, 3 + part : 4 + part, :] = head_mod[
                pl.ds(step, 1), part * model : (part + 1) * model
            ]
        for p in range(patches):
            meta[video, 5 + p : 6 + p, :] = jnp.full((1, model), counts[j, p].astype(jnp.float32))
        lat_stage[j] = latent[j, 0].astype(jnp.bfloat16)
    mine = meta.at[pl.ds(2 * c, 2)]
    meta_copy = remote(mine, mine, meta_send, meta_recv, sibling)
    meta_copy.start()

    def lat_owner_self(j):
        return jnp.logical_and(s == 0, jnp.logical_and(2 * c + j == z, across == c))

    def lat_owner_copy(j):
        return remote(
            lat_stage.at[j],
            lat_owner.at[spot, :, pl.ds(pl.multiple_of(s * half, half), half)],
            lo_send.at[j],
            lo_recv.at[spot, s],
            device(0, 2 * c + j, g, across),
        )

    def lat_home_copy(j):
        return remote(
            lat_stage.at[j],
            lat_home.at[j, :, pl.ds(pl.multiple_of(s * half, half), half)],
            lh_send.at[j],
            lh_recv.at[j, s],
            device(0, z, g, c),
        )

    for j in range(2):

        @pl.when(lat_owner_self(j))
        def _():
            pltpu.make_async_copy(
                lat_stage.at[j],
                lat_owner.at[spot, :, pl.ds(pl.multiple_of(s * half, half), half)],
                lo_recv.at[spot, s],
            ).start()

        @pl.when(jnp.logical_not(lat_owner_self(j)))
        def _():
            lat_owner_copy(j).start()

        @pl.when(s == 1)
        def _():
            lat_home_copy(j).start()

        @pl.when(s == 0)
        def _():
            pltpu.make_async_copy(
                lat_stage.at[j], lat_home.at[j, :, :half], lh_recv.at[j, 0]
            ).start()

    for t in range(4):
        w_own(t).start()
        w_sibling(t).start()

    meta_copy.wait()

    for p in range(patches):
        row = lax.broadcasted_iota(jnp.int32, (slots, HD), 0).astype(jnp.float32)
        live = row < meta[z, 5 + p : 6 + p, :HD]
        live_buf[p] = jnp.where(live, 1.0, 0.0).astype(jnp.bfloat16)

    def weights_arrive(t):
        for dg in range(1, chips):
            w_across(t, dg).wait_recv()
        if t == 0:
            across_start(2)
        for dg in range(1, chips):
            w_forward(t, dg).start()
        w_own(t).wait()
        w_sibling(t).wait_recv()
        for dg in range(1, chips):
            w_forward(t, dg).wait_recv()

    def in_rows(count, step, body, unroll):
        def one(i, carry):
            body(pl.multiple_of(i * step, step))
            return carry

        lax.fori_loop(0, count // step, one, 0, unroll=unroll)

    def mask_rows(p, key_ref, value_ref, base):
        first = key_ref[pl.ds(base, 16), :][0:1, :].astype(jnp.float32)
        last_row = meta[z, pl.ds(5 + p, 1), :]

        def rows_of(at):
            rows = pl.ds(base + at, 16)
            row = lax.broadcasted_iota(jnp.int32, (16, model), 0) + at
            live = row.astype(jnp.float32) < last_row
            key_ref[rows, :] = jnp.where(live, key_ref[rows, :].astype(jnp.float32), first).astype(
                jnp.bfloat16
            )
            value_ref[rows, :] = jnp.where(
                live, value_ref[rows, :].astype(jnp.float32), 0.0
            ).astype(jnp.bfloat16)

        in_rows(slots, 16, rows_of, 2)

    def caches_arrive():
        for p in range(patches):
            kv_arrival(p).wait_recv()
            kv_forward(p).start()
        for p in range(patches):
            kv_forward(p).wait()
            mask_rows(p, kvbuf.at[0, p], kvbuf.at[1, p], 0)

    def multiply(left, weight, sink):
        def tile(i, carry):
            cols = pl.ds(pl.multiple_of(i * TILE, TILE), TILE)
            sink(i, cols, jnp.dot(left[...], weight[:, cols], preferred_element_type=jnp.float32))
            return carry

        lax.fori_loop(0, tiles, tile, 0)

    def embed_rows(lat_ref, base):
        def tile(i, carry):
            cols = pl.ds(pl.multiple_of(i * TILE, TILE), TILE)
            hid[pl.ds(base, slots), cols] = lax.dot_general(
                lat_ref[...],
                embed[:, cols],
                (((0,), (0,)), ((), ())),
                preferred_element_type=jnp.float32,
            )
            return carry

        lax.fori_loop(0, tiles, tile, 0)

    def norm_rows(video, shift_row, scale_row, base):
        shift = meta[video, shift_row : shift_row + 1, :]
        scale = 1.0 + meta[video, scale_row : scale_row + 1, :]

        def rows_of(at):
            rows = pl.ds(base + at, 16)
            values = hid[rows, :]
            center = values - jnp.mean(values, axis=-1, keepdims=True)
            unit = center * lax.rsqrt(jnp.mean(center * center, axis=-1, keepdims=True) + EPS)
            normed[rows, :] = (unit * scale + shift).astype(jnp.bfloat16)

        in_rows(slots, 16, rows_of, 4)

    def rms_rows(out_ref, cols, gain_cols, factor, base, count, live=None):
        gains = gain[:, gain_cols] * factor

        def rows_of(at):
            rows = pl.ds(base + at, 16)
            values = proj[rows, :]
            scaled = values * lax.rsqrt(jnp.mean(values * values, axis=-1, keepdims=True) + EPS)
            scaled = scaled * gains
            if live is not None:
                row = lax.broadcasted_iota(jnp.int32, (16, model), 0) + at
                scaled = jnp.where(row < live, scaled, 0.0)
            out_ref[rows if live is None else pl.ds(at, 16), cols] = scaled.astype(jnp.bfloat16)

        in_rows(count, 16, rows_of, 4)

    def attend(k, base):
        own = 2 * c + k
        mine = pl.ds(base, slots)

        def head(h, carry):
            cols = pl.ds(pl.multiple_of(h * HD, HD), HD)
            query = q_buf[mine, cols]
            scores = []
            for b in range(patches):
                p = lax.rem(own + b, patches)
                keys = k_buf[mine, cols] if b == 0 else kvbuf[0, p, :, cols]
                scores.append(
                    lax.dot_general(
                        query, keys, (((1,), (1,)), ((), ())), preferred_element_type=jnp.float32
                    )
                )
            top = scores[0]
            for score in scores[1:]:
                top = jnp.maximum(top, score)
            top = jnp.max(top, axis=1, keepdims=True)
            mixed = None
            for b in range(patches):
                p = lax.rem(own + b, patches)
                weight = jnp.exp2(scores[b] - top).astype(jnp.bfloat16)
                values = v_buf[mine, cols] if b == 0 else kvbuf[1, p, :, cols]
                both = jnp.concatenate([values, live_buf[p]], axis=1)
                part = jnp.dot(weight, both, preferred_element_type=jnp.float32)
                mixed = part if mixed is None else mixed + part
            attended[:, cols] = (mixed[:, :HD] / mixed[:, HD:]).astype(jnp.bfloat16)
            return carry

        lax.fori_loop(0, HEADS, head, 0, unroll=4)

    def home_of(k, section):
        return device(section, 2 * c + k, g, across)

    def home_is_self(k):
        return jnp.logical_and(2 * c + k == z, across == c)

    def h1_tile(ref, i):
        return ref.at[:, pl.ds(pl.multiple_of(i * TILE, TILE), TILE)]

    def h1_over(k, i):
        return remote(
            h1_tile(h1_stage.at[k], i),
            h1_tile(h1_buf.at[k], i),
            h1_send.at[k, i],
            h1_recv.at[k, i],
            device(1, z, g, c),
        )

    def h1_to_home(k, i):
        return remote(
            h1_tile(h1_buf.at[k], i),
            h1_tile(h1_home.at[spot], i),
            hh_send.at[k, i],
            hh_recv.at[spot, i],
            home_of(k, 1),
        )

    def h1_arrives(k, i):
        h1_over(k, i).wait_recv()

        @pl.when(home_is_self(k))
        def _():
            pltpu.make_async_copy(
                h1_tile(h1_buf.at[k], i), h1_tile(h1_home.at[spot], i), hh_recv.at[spot, i]
            ).start()

        @pl.when(jnp.logical_not(home_is_self(k)))
        def _():
            h1_to_home(k, i).start()

    def vel_src(k, section):
        return vel_stage.at[k, :, section * half : (section + 1) * half]

    def vel_to_home(k, section):
        return remote(
            vel_src(k, section),
            vel_buf.at[spot],
            vel_send.at[k, section],
            vel_recv.at[spot],
            home_of(k, section),
        )

    factor = math.log2(math.e) / math.sqrt(HD)

    def project(t, base, count):
        rows = pl.ds(base, count)

        def sink_proj(i, cols, product):
            proj[rows, cols] = product

        def sink_value(i, cols, product):
            v_buf[rows, cols] = product.astype(jnp.bfloat16)

        multiply(normed.at[rows], wbuf.at[t], sink_value if t == 2 else sink_proj)
        if t == 0:
            rms_rows(q_buf, slice(None), slice(0, model), factor, base, count)
        if t == 1:
            rms_rows(k_buf, slice(None), slice(model, 2 * model), 1.0, base, count)

    def update(k, base, after):
        rows = pl.ds(base, slots)

        def sink_update(i, cols, product):
            after(i, cols, hid[rows, cols] + meta[z, 2:3, cols] * product)

        multiply(attended, wbuf.at[3], sink_update)

    def fresh_out(j):
        return pltpu.make_async_copy(fresh_stage.at[j], fresh.at[0, j, 0], out_sem.at[j])

    def home(j):
        live = counts[j, z]
        norm_rows(2 * c + j, 0, 1, 0)
        first = normed.at[pl.ds(0, slots)]

        def sink_key(i, cols, product):
            proj[pl.ds(0, slots), cols] = product

        multiply(first, wbuf.at[1], sink_key)
        rms_rows(
            fresh_stage.at[j], slice(0, model), slice(model, 2 * model), 1.0, 0, slots, live
        )

        def sink_fresh(i, cols, product):
            row = lax.broadcasted_iota(jnp.int32, product.shape, 0)
            fresh_stage[j, :, pl.ds(pl.multiple_of(model + i * TILE, TILE), TILE)] = jnp.where(
                row < live, product, 0.0
            ).astype(jnp.bfloat16)

        multiply(first, wbuf.at[2], sink_fresh)
        fresh_out(j).start()

    def first_parts():
        parts_first(1)
        parts_first(3)
        across_start(0)
        kv_start(1, 0)
        kv_start(1, 1)

    @pl.when(s == 0)
    def _():
        def enter(k, carry):
            for part in range(2):
                cols = pl.ds(part * half, half)
                remote(
                    lat_owner.at[k, :, cols],
                    lat_owner.at[k, :, cols],
                    lo_send.at[0],
                    lo_recv.at[k, part],
                    sibling,
                ).wait_recv()
            base = pl.multiple_of(k * slots, slots)
            embed_rows(lat_owner.at[k], base)
            norm_rows(z, 0, 1, base)
            return carry

        first_parts()
        lax.fori_loop(0, 2, enter, 0)
        weights_arrive(0)
        project(0, 0, 2 * slots)
        parts_second(1)
        project(1, 0, 2 * slots)
        parts_second(3)
        caches_arrive()
        weights_arrive(2)
        project(2, 0, 2 * slots)

        def leave(turn, carry):
            k = lax.rem(turn + z, 2)
            base = pl.multiple_of(k * slots, slots)
            mask_rows(2 * c + k, k_buf, v_buf, base)
            attend(k, base)

            def after(i, cols, hidden):
                h1_stage[k, :, cols] = hidden.astype(jnp.bfloat16)
                h1_over(k, i).start()

            update(k, base, after)
            return carry

        lax.fori_loop(0, 2, leave, 0)

        def home_first(j, carry):
            for part in range(2):
                cols = pl.ds(part * half, half)
                remote(
                    lat_home.at[j, :, cols],
                    lat_home.at[j, :, cols],
                    lh_send.at[0],
                    lh_recv.at[j, part],
                    sibling,
                ).wait_recv()
            embed_rows(lat_home.at[j], 0)
            home(j)
            return carry

        lax.fori_loop(0, 2, home_first, 0)
        for k in range(2):
            for i in range(tiles):
                h1_over(k, i).wait_send()

    @pl.when(s == 1)
    def _():
        first_parts()
        weights_arrive(0)
        parts_second(1)
        parts_second(3)
        caches_arrive()
        weights_arrive(2)

        def turn_of(turn, carry):
            k = lax.rem(turn + z, 2)
            base = pl.multiple_of(k * slots, slots)
            rows = pl.ds(base, slots)

            @pl.when(turn == 0)
            def _():
                for i in range(tiles):
                    h1_arrives(k, i)

            @pl.when(turn == 1)
            def _():
                h1_arrives(k, tiles - 1)

            hid[rows, :] = h1_buf[k].astype(jnp.float32)
            norm_rows(z, 0, 1, base)
            project(0, base, slots)
            project(1, base, slots)
            project(2, base, slots)

            @pl.when(turn == 0)
            def _():
                h1_arrives(1 - k, 0)

            mask_rows(2 * c + k, k_buf, v_buf, base)
            attend(k, base)

            @pl.when(turn == 0)
            def _():
                h1_arrives(1 - k, 1)

            def after(i, cols, hidden):
                hid[rows, cols] = hidden

            update(k, base, after)
            norm_rows(z, 3, 4, base)
            vel_stage[k] = lax.dot_general(
                head_weight[...],
                normed[rows, :],
                (((1,), (1,)), ((), ())),
                preferred_element_type=jnp.float32,
            )
            vel_to_home(k, 0).start()

            @pl.when(home_is_self(k))
            def _():
                pltpu.make_async_copy(vel_src(k, 1), vel_buf.at[spot], vel_recv.at[spot]).start()

            @pl.when(jnp.logical_not(home_is_self(k)))
            def _():
                vel_to_home(k, 1).start()

            j = lax.rem(turn + z, 2)
            for i in range(tiles):
                remote(
                    h1_tile(h1_home.at[j], i),
                    h1_tile(h1_home.at[j], i),
                    hh_send.at[0, i],
                    hh_recv.at[j, i],
                    sibling,
                ).wait_recv()
            hid[pl.ds(0, slots), :] = h1_home[j].astype(jnp.float32)
            home(j)
            return carry

        lax.fori_loop(0, 2, turn_of, 0)
        for k in range(2):
            vel_to_home(k, 0).wait_send()

            @pl.when(jnp.logical_not(home_is_self(k)))
            def _():
                for i in range(tiles):
                    h1_to_home(k, i).wait_send()
                vel_to_home(k, 1).wait_send()

    for t in range(4):
        for dg in range(1, chips):
            w_across(t, dg).wait_send()
            if t not in SHARED:
                w_forward(t, dg).wait_send()
        w_sibling(t).wait_send()
    parts_sent()
    for j in range(2):
        for x in range(2):

            @pl.when(jnp.logical_not(kv_is_self(j, x)))
            def _():
                kv_remote(j, x).wait_send()

        @pl.when(jnp.logical_not(lat_owner_self(j)))
        def _():
            lat_owner_copy(j).wait_send()

        @pl.when(s == 1)
        def _():
            lat_home_copy(j).wait_send()

    for j in range(2):
        remote(
            vel_buf.at[j], vel_buf.at[j], vel_send.at[0, 0], vel_recv.at[j], sibling
        ).wait_recv()
        slot = lax.broadcasted_iota(jnp.int32, vel_buf.shape[1:], 1) + s * half
        step = jnp.full(vel_buf.shape[1:], steps[j].astype(jnp.float32))
        value = jnp.where(slot < counts[j, z], vel_buf[j], 0.0)
        velocity[j, 0] = value
        new_latent[j, 0] = latent[j, 0] + (sigma_of(step + 1.0) - sigma_of(step)) * value
        fresh_out(j).wait()


def body(
    chips,
    latent,
    counts,
    steps_idx,
    embed_weight,
    wqkv,
    wo,
    qk_gain,
    modulation,
    head_mod,
    head_weight,
    stale_cache,
):
    videos, _, half, channels = latent.shape
    patches = counts.shape[1]
    slots = stale_cache.shape[3]
    model = embed_weight.shape[1]
    assert videos == 2 and patches == 4
    bf16, f32 = jnp.bfloat16, jnp.float32
    vmem = pl.BlockSpec(memory_space=pltpu.VMEM)
    smem = pl.BlockSpec(memory_space=pltpu.SMEM)
    anywhere = pl.BlockSpec(memory_space=pl.ANY)
    dma = pltpu.SemaphoreType.DMA
    latent = jnp.swapaxes(latent, 2, 3)
    velocity, new_latent, fresh = pl.pallas_call(
        functools.partial(step_kernel, chips),
        in_specs=[vmem, smem, smem, vmem, vmem, vmem, vmem, vmem, anywhere, anywhere, anywhere],
        out_specs=[vmem, vmem, anywhere],
        out_shape=[
            jax.ShapeDtypeStruct(latent.shape, f32),
            jax.ShapeDtypeStruct(latent.shape, f32),
            jax.ShapeDtypeStruct(stale_cache.shape, bf16),
        ],
        scratch_shapes=[
            pltpu.VMEM((4, model, model), bf16),
            pltpu.VMEM((2, patches, slots, model), bf16),
            pltpu.VMEM((patches, slots, HD), bf16),
            pltpu.VMEM((4, META_ROWS, model), f32),
            pltpu.VMEM((2, channels, half), bf16),
            pltpu.VMEM((2, channels, slots), bf16),
            pltpu.VMEM((2, channels, slots), bf16),
            pltpu.VMEM((2 * slots, model), f32),
            pltpu.VMEM((2 * slots, model), f32),
            pltpu.VMEM((2 * slots, model), bf16),
            pltpu.VMEM((2 * slots, model), bf16),
            pltpu.VMEM((2 * slots, model), bf16),
            pltpu.VMEM((2 * slots, model), bf16),
            pltpu.VMEM((slots, model), bf16),
            pltpu.VMEM((2, slots, model), bf16),
            pltpu.VMEM((2, slots, model), bf16),
            pltpu.VMEM((2, slots, model), bf16),
            pltpu.VMEM((2, slots, 2 * model), bf16),
            pltpu.VMEM((2, channels, slots), f32),
            pltpu.VMEM((2, channels, half), f32),
            dma((4,)),
            dma((4, chips)),
            dma((4, chips)),
            dma((4,)),
            dma((4,)),
            dma((3, chips)),
            dma((3, chips)),
            dma((2, chips)),
            dma((2, chips)),
            dma((2, chips, 2)),
            dma((2, chips, 2)),
            dma((2, 2)),
            dma((patches,)),
            dma((patches,)),
            dma((patches,)),
            dma,
            dma,
            dma((2,)),
            dma((2, 2)),
            dma((2,)),
            dma((2, 2)),
            dma((2, model // TILE)),
            dma((2, model // TILE)),
            dma((2, model // TILE)),
            dma((2, model // TILE)),
            dma((2, 2)),
            dma((2,)),
            dma((2,)),
        ],
        compiler_params=pltpu.CompilerParams(
            collective_id=0, has_side_effects=True, vmem_limit_bytes=58 * 1024 * 1024
        ),
    )(
        latent,
        counts,
        steps_idx,
        embed_weight,
        qk_gain,
        jnp.swapaxes(modulation, 0, 1),
        head_mod,
        head_weight.T,
        wqkv,
        wo,
        stale_cache,
    )
    return jnp.swapaxes(velocity, 2, 3), jnp.swapaxes(new_latent, 2, 3), fresh


def solution(mesh):
    chips = mesh.shape["fsdp"] // 2
    in_specs = (
        P("fsdp", "patch", "section", None),
        P("fsdp", None),
        P("fsdp"),
        P(),
        P("section", "fsdp", None),
        P("section", "fsdp", None),
        P("section", None),
        P("section", None, None),
        P(),
        P(),
        P("section", "fsdp", "patch", None, None),
    )
    out_specs = (
        P("fsdp", "patch", "section", None),
        P("fsdp", "patch", "section", None),
        P("section", "fsdp", "patch", None, None),
    )
    return jax.shard_map(
        functools.partial(body, chips),
        mesh=mesh,
        in_specs=in_specs,
        out_specs=out_specs,
        check_vma=False,
    )
```

```python
import functools
import math

import jax
import jax.numpy as jnp
from jax import lax
from jax.experimental import pallas as pl
from jax.experimental.pallas import tpu as pltpu
from jax.sharding import PartitionSpec as P

HEADS = 12
HD = 128
TSTEPS = 50
EPS = 1e-06
MESH = pl.DeviceIdType.MESH
TILE = 512
META_ROWS = 16
SHARED = {1: 0, 3: 1}


def sigma_of(step_float):
    remain = 1.0 - step_float / TSTEPS
    return 5.0 * remain / (1.0 + 4.0 * remain)


def remote(src, dst, send_sem, recv_sem, target):
    return pltpu.make_async_remote_copy(
        src_ref=src,
        dst_ref=dst,
        send_sem=send_sem,
        recv_sem=recv_sem,
        device_id=target,
        device_id_type=MESH,
    )


def step_kernel(
    chips,
    latent,
    counts,
    steps,
    gain,
    embed_in,
    modulation_in,
    head_mod_in,
    head_weight_in,
    wqkv,
    wo,
    stale,
    velocity,
    new_latent,
    fresh,
    embed,
    modulation,
    head_mod,
    head_weight,
    table_sem,
    value_sem,
    wbuf,
    kvbuf,
    live_buf,
    meta,
    lat_stage,
    lat_owner,
    lat_home,
    hid,
    proj,
    normed,
    q_buf,
    k_buf,
    v_buf,
    attended,
    h1_stage,
    h1_buf,
    h1_home,
    fresh_stage,
    vel_stage,
    vel_buf,
    w_local,
    wy_send,
    wy_recv,
    ws_send,
    ws_recv,
    wf_send,
    wf_recv,
    zr_send,
    zr_recv,
    zf_send,
    zf_recv,
    kv_send,
    kv_recv,
    kf_send,
    kf_recv,
    meta_send,
    meta_recv,
    lo_send,
    lo_recv,
    lh_send,
    lh_recv,
    h1_send,
    h1_recv,
    hh_send,
    hh_recv,
    vel_send,
    vel_recv,
    out_sem,
):
    s = lax.axis_index("section")
    z = lax.axis_index("patch")
    f = lax.axis_index("fsdp")
    c = lax.rem(f, 2)
    g = f // 2
    model = embed.shape[1]
    shard_rows = wqkv.shape[1]
    slots = kvbuf.shape[2]
    half = slots // 2
    part_cols = model // 2
    tiles = model // TILE
    patches = kvbuf.shape[1]

    def device(section, patch, chip, core):
        return {"section": section, "patch": patch, "fsdp": 2 * chip + core}

    sibling = device(s, z, g, 1 - c)
    tables = [
        pltpu.make_async_copy(src, dst, table_sem.at[i])
        for i, (src, dst) in enumerate(
            [
                (modulation_in, modulation),
                (head_mod_in, head_mod),
                (embed_in, embed),
                (head_weight_in, head_weight),
            ]
        )
    ]
    across = z // 2
    spot = lax.rem(z, 2)

    barrier = pltpu.get_barrier_semaphore()
    greeted = 0
    for ds in range(2):
        for dz in range(patches):
            for dc in range(2):
                if ds or dz or dc:
                    pl.semaphore_signal(
                        barrier,
                        inc=1,
                        device_id=device(
                            lax.rem(s + ds, 2), lax.rem(z + dz, patches), g, lax.rem(c + dc, 2)
                        ),
                        device_id_type=MESH,
                    )
                    greeted += 1
    for dg in range(1, chips):
        pl.semaphore_signal(
            barrier, inc=1, device_id=device(s, z, lax.rem(g + dg, chips), c), device_id_type=MESH
        )
        greeted += 1
    pl.semaphore_wait(barrier, greeted)

    def weight_src(t):
        if t < 3:
            return wqkv.at[0, :, t * model : (t + 1) * model]
        return wo.at[0]

    def weight_rows(t, owner):
        return wbuf.at[t, pl.ds(pl.multiple_of(owner * shard_rows, shard_rows), shard_rows), :]

    def w_own(t):
        return pltpu.make_async_copy(weight_src(t), weight_rows(t, f), w_local.at[t])

    def cols_of(q, start=0):
        return pl.ds(pl.multiple_of(start + q * part_cols, part_cols), part_cols)

    def owner_back(dg):
        return 2 * lax.rem(g + chips - dg, chips) + c

    def w_across(t, dg):
        src, dst = weight_src(t), weight_rows(t, f)
        if t in SHARED:
            src = wo.at[0, :, cols_of(spot)] if t == 3 else wqkv.at[0, :, cols_of(spot, t * model)]
            dst = part_of(t, 0, spot)
        return remote(
            src,
            dst,
            wy_send.at[t, dg],
            wy_recv.at[t, dg],
            device(s, z, lax.rem(g + dg, chips), c),
        )

    def part_of(t, dg, q):
        rows = pl.ds(pl.multiple_of(owner_back(dg) * shard_rows, shard_rows), shard_rows)
        return wbuf.at[t, rows, cols_of(q)]

    def part_forward(t, dg, q):
        part, at = part_of(t, dg, q), SHARED[t]
        return remote(part, part, zf_send.at[at, dg, q], zf_recv.at[at, dg, q], sibling)

    def part_pair(t, dg, q):
        part, at = part_of(t, dg, q), SHARED[t]
        return remote(
            part, part, zr_send.at[at, dg], zr_recv.at[at, dg], device(s, z + 1 - 2 * spot, g, c)
        )

    def parts_first(t):
        for dg in range(1, chips):
            w_across(t, dg).wait_recv()
            part_pair(t, dg, spot).start()
            part_forward(t, dg, spot).start()

    def parts_second(t):
        for dg in range(1, chips):
            part_pair(t, dg, 1 - spot).wait_recv()
            part_forward(t, dg, 1 - spot).start()
        w_own(t).wait()
        w_sibling(t).wait_recv()
        for dg in range(1, chips):
            for q in range(2):
                part_forward(t, dg, q).wait_recv()

    def parts_sent():
        for t in SHARED:
            for dg in range(1, chips):
                part_pair(t, dg, spot).wait_send()
                for q in range(2):
                    part_forward(t, dg, q).wait_send()

    def w_sibling(t):
        return remote(weight_src(t), weight_rows(t, f), ws_send.at[t], ws_recv.at[t], sibling)

    def w_forward(t, dg):
        rows = weight_rows(t, 2 * lax.rem(g + chips - dg, chips) + c)
        return remote(rows, rows, wf_send.at[t, dg], wf_recv.at[t, dg], sibling)

    def kv_src(j, x):
        if x == 1:
            return fresh_stage.at[j, :, model:]
        return stale.at[0, j, 0, :, :model]

    def value_in(j):
        return pltpu.make_async_copy(
            stale.at[0, j, 0, :, model:], fresh_stage.at[j, :, model:], value_sem.at[j]
        )

    def kv_is_self(j, x):
        return jnp.logical_and(2 * c + j == z, c == x)

    def kv_remote(j, x):
        return remote(
            kv_src(j, x),
            kvbuf.at[x, z],
            kv_send.at[j, x],
            kv_recv.at[z],
            device(s, 2 * c + j, g, x),
        )

    def kv_arrival(p):
        return remote(kvbuf.at[c, p], kvbuf.at[c, p], kf_send.at[p], kv_recv.at[p], sibling)

    def kv_forward(p):
        return remote(kvbuf.at[c, p], kvbuf.at[c, p], kf_send.at[p], kf_recv.at[p], sibling)

    def kv_start(j, x):
        @pl.when(kv_is_self(j, x))
        def _():
            pltpu.make_async_copy(kv_src(j, x), kvbuf.at[x, z], kv_recv.at[z]).start()

        @pl.when(jnp.logical_not(kv_is_self(j, x)))
        def _():
            kv_remote(j, x).start()

    def across_start(t):
        for dg in range(1, chips):
            w_across(t, dg).start()

    across_start(1)
    across_start(3)
    kv_start(0, 0)
    kv_start(1, 0)
    for table in tables:
        table.start()
    for j in range(2):
        value_in(j).start()
    for table in tables:
        table.wait()

    for j in range(2):
        step = steps[j]
        video = 2 * c + j
        for part in range(3):
            meta[video, part : part + 1, :] = modulation[
                step, :, part * model : (part + 1) * model
            ]
        for part in range(2):
            meta[video, 3 + part : 4 + part, :] = head_mod[
                pl.ds(step, 1), part * model : (part + 1) * model
            ]
        for p in range(patches):
            meta[video, 5 + p : 6 + p, :] = jnp.full((1, model), counts[j, p].astype(jnp.float32))
        lat_stage[j] = latent[j, 0].astype(jnp.bfloat16)
    mine = meta.at[pl.ds(2 * c, 2)]
    meta_copy = remote(mine, mine, meta_send, meta_recv, sibling)
    meta_copy.start()

    def lat_owner_self(j):
        return jnp.logical_and(s == 0, jnp.logical_and(2 * c + j == z, across == c))

    def lat_owner_copy(j):
        return remote(
            lat_stage.at[j],
            lat_owner.at[spot, :, pl.ds(pl.multiple_of(s * half, half), half)],
            lo_send.at[j],
            lo_recv.at[spot, s],
            device(0, 2 * c + j, g, across),
        )

    def lat_home_copy(j):
        return remote(
            lat_stage.at[j],
            lat_home.at[j, :, pl.ds(pl.multiple_of(s * half, half), half)],
            lh_send.at[j],
            lh_recv.at[j, s],
            device(0, z, g, c),
        )

    for j in range(2):

        @pl.when(lat_owner_self(j))
        def _():
            pltpu.make_async_copy(
                lat_stage.at[j],
                lat_owner.at[spot, :, pl.ds(pl.multiple_of(s * half, half), half)],
                lo_recv.at[spot, s],
            ).start()

        @pl.when(jnp.logical_not(lat_owner_self(j)))
        def _():
            lat_owner_copy(j).start()

        @pl.when(s == 1)
        def _():
            lat_home_copy(j).start()

        @pl.when(s == 0)
        def _():
            pltpu.make_async_copy(
                lat_stage.at[j], lat_home.at[j, :, :half], lh_recv.at[j, 0]
            ).start()

    for t in range(4):
        w_own(t).start()
        w_sibling(t).start()

    meta_copy.wait()

    for p in range(patches):
        row = lax.broadcasted_iota(jnp.int32, (slots, HD), 0).astype(jnp.float32)
        live = row < meta[z, 5 + p : 6 + p, :HD]
        live_buf[p] = jnp.where(live, 1.0, 0.0).astype(jnp.bfloat16)

    def weights_arrive(t):
        for dg in range(1, chips):
            w_across(t, dg).wait_recv()
        if t == 0:
            across_start(2)
        for dg in range(1, chips):
            w_forward(t, dg).start()
        w_own(t).wait()
        w_sibling(t).wait_recv()
        for dg in range(1, chips):
            w_forward(t, dg).wait_recv()

    def in_rows(count, step, body, unroll):
        def one(i, carry):
            body(pl.multiple_of(i * step, step))
            return carry

        lax.fori_loop(0, count // step, one, 0, unroll=unroll)

    def mask_keys(p, key_ref, base):
        first = key_ref[pl.ds(base, 16), :][0:1, :].astype(jnp.float32)
        last_row = meta[z, pl.ds(5 + p, 1), :]

        def rows_of(at):
            rows = pl.ds(base + at, 16)
            row = lax.broadcasted_iota(jnp.int32, (16, model), 0) + at
            live = row.astype(jnp.float32) < last_row
            key_ref[rows, :] = jnp.where(live, key_ref[rows, :].astype(jnp.float32), first).astype(
                jnp.bfloat16
            )

        in_rows(slots, 16, rows_of, 4)

    def mask_values(value_ref, base, live):
        def rows_of(at):
            rows = pl.ds(base + at, 16)
            row = lax.broadcasted_iota(jnp.int32, (16, model), 0) + at
            value_ref[rows, :] = jnp.where(
                row.astype(jnp.float32) < live, value_ref[rows, :].astype(jnp.float32), 0.0
            ).astype(jnp.bfloat16)

        in_rows(slots, 16, rows_of, 4)

    def values_ready():
        for j in range(2):
            value_in(j).wait()
            mask_values(fresh_stage.at[j, :, model:], 0, counts[j, z].astype(jnp.float32))

    def keys_early():
        @pl.when(c == 0)
        def _():
            for p in range(patches):
                kv_arrival(p).wait_recv()
                kv_forward(p).start()
            for p in range(patches):
                kv_forward(p).wait_send()
                mask_keys(p, kvbuf.at[0, p], 0)

    def caches_arrive():
        @pl.when(c == 1)
        def _():
            for p in range(patches):
                kv_forward(p).wait_recv()
                mask_keys(p, kvbuf.at[0, p], 0)
            for p in range(patches):
                kv_arrival(p).wait_recv()
                kv_forward(p).start()
            for p in range(patches):
                kv_forward(p).wait_send()

        @pl.when(c == 0)
        def _():
            for p in range(patches):
                kv_forward(p).wait_recv()

    def kv_sent():
        for j in range(2):
            for x in range(2):

                @pl.when(jnp.logical_not(kv_is_self(j, x)))
                def _():
                    kv_remote(j, x).wait_send()

    def multiply(left, weight, sink):
        def tile(i, carry):
            cols = pl.ds(pl.multiple_of(i * TILE, TILE), TILE)
            sink(i, cols, jnp.dot(left[...], weight[:, cols], preferred_element_type=jnp.float32))
            return carry

        lax.fori_loop(0, tiles, tile, 0)

    def embed_rows(lat_ref, base):
        def tile(i, carry):
            cols = pl.ds(pl.multiple_of(i * TILE, TILE), TILE)
            hid[pl.ds(base, slots), cols] = lax.dot_general(
                lat_ref[...],
                embed[:, cols],
                (((0,), (0,)), ((), ())),
                preferred_element_type=jnp.float32,
            )
            return carry

        lax.fori_loop(0, tiles, tile, 0)

    def norm_rows(video, shift_row, scale_row, base):
        shift = meta[video, shift_row : shift_row + 1, :]
        scale = 1.0 + meta[video, scale_row : scale_row + 1, :]

        def rows_of(at):
            rows = pl.ds(base + at, 16)
            values = hid[rows, :]
            center = values - jnp.mean(values, axis=-1, keepdims=True)
            unit = center * lax.rsqrt(jnp.mean(center * center, axis=-1, keepdims=True) + EPS)
            normed[rows, :] = (unit * scale + shift).astype(jnp.bfloat16)

        in_rows(slots, 16, rows_of, 4)

    def rms_rows(out_ref, cols, gain_cols, factor, base, count, live=None):
        gains = gain[:, gain_cols] * factor

        def rows_of(at):
            rows = pl.ds(base + at, 16)
            values = proj[rows, :]
            scaled = values * lax.rsqrt(jnp.mean(values * values, axis=-1, keepdims=True) + EPS)
            scaled = scaled * gains
            if live is not None:
                row = lax.broadcasted_iota(jnp.int32, (16, model), 0) + at
                scaled = jnp.where(row < live, scaled, 0.0)
            out_ref[rows if live is None else pl.ds(at, 16), cols] = scaled.astype(jnp.bfloat16)

        in_rows(count, 16, rows_of, 4)

    def attend(k, base):
        own = 2 * c + k
        mine = pl.ds(base, slots)

        def head(h, carry):
            cols = pl.ds(pl.multiple_of(h * HD, HD), HD)
            query = q_buf[mine, cols]
            scores = []
            for b in range(patches):
                p = lax.rem(own + b, patches)
                keys = k_buf[mine, cols] if b == 0 else kvbuf[0, p, :, cols]
                scores.append(
                    lax.dot_general(
                        query, keys, (((1,), (1,)), ((), ())), preferred_element_type=jnp.float32
                    )
                )
            top = scores[0]
            for score in scores[1:]:
                top = jnp.maximum(top, score)
            top = jnp.max(top, axis=1, keepdims=True)
            mixed = None
            for b in range(patches):
                p = lax.rem(own + b, patches)
                weight = jnp.exp2(scores[b] - top).astype(jnp.bfloat16)
                values = v_buf[mine, cols] if b == 0 else kvbuf[1, p, :, cols]
                both = jnp.concatenate([values, live_buf[p]], axis=1)
                part = jnp.dot(weight, both, preferred_element_type=jnp.float32)
                mixed = part if mixed is None else mixed + part
            attended[:, cols] = (mixed[:, :HD] / mixed[:, HD:]).astype(jnp.bfloat16)
            return carry

        lax.fori_loop(0, HEADS, head, 0, unroll=4)

    def home_of(k, section):
        return device(section, 2 * c + k, g, across)

    def home_is_self(k):
        return jnp.logical_and(2 * c + k == z, across == c)

    def h1_tile(ref, i):
        return ref.at[:, pl.ds(pl.multiple_of(i * TILE, TILE), TILE)]

    def h1_over(k, i):
        return remote(
            h1_tile(h1_stage.at[k], i),
            h1_tile(h1_buf.at[k], i),
            h1_send.at[k, i],
            h1_recv.at[k, i],
            device(1, z, g, c),
        )

    def h1_to_home(k, i):
        return remote(
            h1_tile(h1_buf.at[k], i),
            h1_tile(h1_home.at[spot], i),
            hh_send.at[k, i],
            hh_recv.at[spot, i],
            home_of(k, 1),
        )

    def h1_arrives(k, i):
        h1_over(k, i).wait_recv()

        @pl.when(home_is_self(k))
        def _():
            pltpu.make_async_copy(
                h1_tile(h1_buf.at[k], i), h1_tile(h1_home.at[spot], i), hh_recv.at[spot, i]
            ).start()

        @pl.when(jnp.logical_not(home_is_self(k)))
        def _():
            h1_to_home(k, i).start()

    def vel_src(k, section):
        return vel_stage.at[k, :, section * half : (section + 1) * half]

    def vel_to_home(k, section):
        return remote(
            vel_src(k, section),
            vel_buf.at[spot],
            vel_send.at[k, section],
            vel_recv.at[spot],
            home_of(k, section),
        )

    factor = math.log2(math.e) / math.sqrt(HD)

    def project(t, base, count):
        rows = pl.ds(base, count)

        def sink_proj(i, cols, product):
            proj[rows, cols] = product

        def sink_value(i, cols, product):
            v_buf[rows, cols] = product.astype(jnp.bfloat16)

        multiply(normed.at[rows], wbuf.at[t], sink_value if t == 2 else sink_proj)
        if t == 0:
            rms_rows(q_buf, slice(None), slice(0, model), factor, base, count)
        if t == 1:
            rms_rows(k_buf, slice(None), slice(model, 2 * model), 1.0, base, count)

    def update(k, base, after):
        rows = pl.ds(base, slots)

        def sink_update(i, cols, product):
            after(i, cols, hid[rows, cols] + meta[z, 2:3, cols] * product)

        multiply(attended, wbuf.at[3], sink_update)

    def fresh_out(j):
        return pltpu.make_async_copy(fresh_stage.at[j], fresh.at[0, j, 0], out_sem.at[j])

    def home(j):
        live = counts[j, z]
        norm_rows(2 * c + j, 0, 1, 0)
        first = normed.at[pl.ds(0, slots)]

        def sink_key(i, cols, product):
            proj[pl.ds(0, slots), cols] = product

        multiply(first, wbuf.at[1], sink_key)
        rms_rows(
            fresh_stage.at[j], slice(0, model), slice(model, 2 * model), 1.0, 0, slots, live
        )

        def sink_fresh(i, cols, product):
            row = lax.broadcasted_iota(jnp.int32, product.shape, 0)
            fresh_stage[j, :, pl.ds(pl.multiple_of(model + i * TILE, TILE), TILE)] = jnp.where(
                row < live, product, 0.0
            ).astype(jnp.bfloat16)

        multiply(first, wbuf.at[2], sink_fresh)
        fresh_out(j).start()

    def first_parts():
        parts_first(1)
        parts_first(3)
        across_start(0)
        kv_start(0, 1)
        kv_start(1, 1)

    @pl.when(s == 0)
    def _():
        def enter(k, carry):
            for part in range(2):
                cols = pl.ds(part * half, half)
                remote(
                    lat_owner.at[k, :, cols],
                    lat_owner.at[k, :, cols],
                    lo_send.at[0],
                    lo_recv.at[k, part],
                    sibling,
                ).wait_recv()
            base = pl.multiple_of(k * slots, slots)
            embed_rows(lat_owner.at[k], base)
            norm_rows(z, 0, 1, base)
            return carry

        values_ready()
        first_parts()
        lax.fori_loop(0, 2, enter, 0)
        weights_arrive(0)
        project(0, 0, 2 * slots)
        keys_early()
        parts_second(1)
        project(1, 0, 2 * slots)
        parts_second(3)
        caches_arrive()
        weights_arrive(2)
        project(2, 0, 2 * slots)

        def leave(turn, carry):
            k = lax.rem(turn + z, 2)
            base = pl.multiple_of(k * slots, slots)
            mask_keys(2 * c + k, k_buf, base)
            mask_values(v_buf, base, meta[z, pl.ds(5 + 2 * c + k, 1), :])
            attend(k, base)

            def after(i, cols, hidden):
                h1_stage[k, :, cols] = hidden.astype(jnp.bfloat16)
                h1_over(k, i).start()

            update(k, base, after)
            return carry

        lax.fori_loop(0, 2, leave, 0)

        def home_first(j, carry):
            for part in range(2):
                cols = pl.ds(part * half, half)
                remote(
                    lat_home.at[j, :, cols],
                    lat_home.at[j, :, cols],
                    lh_send.at[0],
                    lh_recv.at[j, part],
                    sibling,
                ).wait_recv()
            embed_rows(lat_home.at[j], 0)
            home(j)
            return carry

        kv_sent()
        lax.fori_loop(0, 2, home_first, 0)
        for k in range(2):
            for i in range(tiles):
                h1_over(k, i).wait_send()

    @pl.when(s == 1)
    def _():
        values_ready()
        first_parts()
        weights_arrive(0)
        keys_early()
        parts_second(1)
        parts_second(3)
        caches_arrive()
        weights_arrive(2)

        def turn_of(turn, carry):
            k = lax.rem(turn + z, 2)
            base = pl.multiple_of(k * slots, slots)
            rows = pl.ds(base, slots)

            @pl.when(turn == 0)
            def _():
                for i in range(tiles):
                    h1_arrives(k, i)

            @pl.when(turn == 1)
            def _():
                h1_arrives(k, tiles - 1)

            hid[rows, :] = h1_buf[k].astype(jnp.float32)
            norm_rows(z, 0, 1, base)
            project(0, base, slots)
            project(1, base, slots)
            project(2, base, slots)

            @pl.when(turn == 0)
            def _():
                h1_arrives(1 - k, 0)

            mask_keys(2 * c + k, k_buf, base)
            mask_values(v_buf, base, meta[z, pl.ds(5 + 2 * c + k, 1), :])
            attend(k, base)

            @pl.when(turn == 0)
            def _():
                h1_arrives(1 - k, 1)

            def after(i, cols, hidden):
                hid[rows, cols] = hidden

            update(k, base, after)
            norm_rows(z, 3, 4, base)
            vel_stage[k] = lax.dot_general(
                head_weight[...],
                normed[rows, :],
                (((1,), (1,)), ((), ())),
                preferred_element_type=jnp.float32,
            )
            vel_to_home(k, 0).start()

            @pl.when(home_is_self(k))
            def _():
                pltpu.make_async_copy(vel_src(k, 1), vel_buf.at[spot], vel_recv.at[spot]).start()

            @pl.when(jnp.logical_not(home_is_self(k)))
            def _():
                vel_to_home(k, 1).start()

            j = lax.rem(turn + z, 2)
            for i in range(tiles):
                remote(
                    h1_tile(h1_home.at[j], i),
                    h1_tile(h1_home.at[j], i),
                    hh_send.at[0, i],
                    hh_recv.at[j, i],
                    sibling,
                ).wait_recv()
            hid[pl.ds(0, slots), :] = h1_home[j].astype(jnp.float32)
            home(j)
            return carry

        kv_sent()
        lax.fori_loop(0, 2, turn_of, 0)
        for k in range(2):
            vel_to_home(k, 0).wait_send()

            @pl.when(jnp.logical_not(home_is_self(k)))
            def _():
                for i in range(tiles):
                    h1_to_home(k, i).wait_send()
                vel_to_home(k, 1).wait_send()

    for t in range(4):
        for dg in range(1, chips):
            w_across(t, dg).wait_send()
            if t not in SHARED:
                w_forward(t, dg).wait_send()
        w_sibling(t).wait_send()
    parts_sent()
    for j in range(2):

        @pl.when(jnp.logical_not(lat_owner_self(j)))
        def _():
            lat_owner_copy(j).wait_send()

        @pl.when(s == 1)
        def _():
            lat_home_copy(j).wait_send()

    for j in range(2):
        remote(
            vel_buf.at[j], vel_buf.at[j], vel_send.at[0, 0], vel_recv.at[j], sibling
        ).wait_recv()
        slot = lax.broadcasted_iota(jnp.int32, vel_buf.shape[1:], 1) + s * half
        step = jnp.full(vel_buf.shape[1:], steps[j].astype(jnp.float32))
        value = jnp.where(slot < counts[j, z], vel_buf[j], 0.0)
        velocity[j, 0] = value
        new_latent[j, 0] = latent[j, 0] + (sigma_of(step + 1.0) - sigma_of(step)) * value
        fresh_out(j).wait()


def body(
    chips,
    latent,
    counts,
    steps_idx,
    embed_weight,
    wqkv,
    wo,
    qk_gain,
    modulation,
    head_mod,
    head_weight,
    stale_cache,
):
    videos, _, half, channels = latent.shape
    patches = counts.shape[1]
    slots = stale_cache.shape[3]
    model = embed_weight.shape[1]
    assert videos == 2 and patches == 4
    bf16, f32 = jnp.bfloat16, jnp.float32
    vmem = pl.BlockSpec(memory_space=pltpu.VMEM)
    smem = pl.BlockSpec(memory_space=pltpu.SMEM)
    anywhere = pl.BlockSpec(memory_space=pl.ANY)
    dma = pltpu.SemaphoreType.DMA
    latent = jnp.swapaxes(latent, 2, 3)
    velocity, new_latent, fresh = pl.pallas_call(
        functools.partial(step_kernel, chips),
        in_specs=[vmem, smem, smem, vmem] + [anywhere] * 7,
        out_specs=[vmem, vmem, anywhere],
        out_shape=[
            jax.ShapeDtypeStruct(latent.shape, f32),
            jax.ShapeDtypeStruct(latent.shape, f32),
            jax.ShapeDtypeStruct(stale_cache.shape, bf16),
        ],
        scratch_shapes=[
            pltpu.VMEM(embed_weight.shape, bf16),
            pltpu.VMEM((modulation.shape[1], 1, 3 * model), f32),
            pltpu.VMEM(head_mod.shape, f32),
            pltpu.VMEM((channels, model), bf16),
            dma((4,)),
            dma((2,)),
            pltpu.VMEM((4, model, model), bf16),
            pltpu.VMEM((2, patches, slots, model), bf16),
            pltpu.VMEM((patches, slots, HD), bf16),
            pltpu.VMEM((4, META_ROWS, model), f32),
            pltpu.VMEM((2, channels, half), bf16),
            pltpu.VMEM((2, channels, slots), bf16),
            pltpu.VMEM((2, channels, slots), bf16),
            pltpu.VMEM((2 * slots, model), f32),
            pltpu.VMEM((2 * slots, model), f32),
            pltpu.VMEM((2 * slots, model), bf16),
            pltpu.VMEM((2 * slots, model), bf16),
            pltpu.VMEM((2 * slots, model), bf16),
            pltpu.VMEM((2 * slots, model), bf16),
            pltpu.VMEM((slots, model), bf16),
            pltpu.VMEM((2, slots, model), bf16),
            pltpu.VMEM((2, slots, model), bf16),
            pltpu.VMEM((2, slots, model), bf16),
            pltpu.VMEM((2, slots, 2 * model), bf16),
            pltpu.VMEM((2, channels, slots), f32),
            pltpu.VMEM((2, channels, half), f32),
            dma((4,)),
            dma((4, chips)),
            dma((4, chips)),
            dma((4,)),
            dma((4,)),
            dma((3, chips)),
            dma((3, chips)),
            dma((2, chips)),
            dma((2, chips)),
            dma((2, chips, 2)),
            dma((2, chips, 2)),
            dma((2, 2)),
            dma((patches,)),
            dma((patches,)),
            dma((patches,)),
            dma,
            dma,
            dma((2,)),
            dma((2, 2)),
            dma((2,)),
            dma((2, 2)),
            dma((2, model // TILE)),
            dma((2, model // TILE)),
            dma((2, model // TILE)),
            dma((2, model // TILE)),
            dma((2, 2)),
            dma((2,)),
            dma((2,)),
        ],
        compiler_params=pltpu.CompilerParams(
            collective_id=0, has_side_effects=True, vmem_limit_bytes=58 * 1024 * 1024
        ),
    )(
        latent,
        counts,
        steps_idx,
        qk_gain,
        embed_weight,
        jnp.swapaxes(modulation, 0, 1),
        head_mod,
        head_weight.T,
        wqkv,
        wo,
        stale_cache,
    )
    return jnp.swapaxes(velocity, 2, 3), jnp.swapaxes(new_latent, 2, 3), fresh


def solution(mesh):
    chips = mesh.shape["fsdp"] // 2
    in_specs = (
        P("fsdp", "patch", "section", None),
        P("fsdp", None),
        P("fsdp"),
        P(),
        P("section", "fsdp", None),
        P("section", "fsdp", None),
        P("section", None),
        P("section", None, None),
        P(),
        P(),
        P("section", "fsdp", "patch", None, None),
    )
    out_specs = (
        P("fsdp", "patch", "section", None),
        P("fsdp", "patch", "section", None),
        P("section", "fsdp", "patch", None, None),
    )
    return jax.shard_map(
        functools.partial(body, chips),
        mesh=mesh,
        in_specs=in_specs,
        out_specs=out_specs,
        check_vma=False,
    )
```

```python
import functools
import math

import jax
import jax.numpy as jnp
from jax import lax
from jax.experimental import pallas as pl
from jax.experimental.pallas import tpu as pltpu
from jax.sharding import PartitionSpec as P

HEADS = 12
HD = 128
TSTEPS = 50
EPS = 1e-06
MESH = pl.DeviceIdType.MESH
TILE = 512
META_ROWS = 16
SHARED = {1: 0, 3: 1}


def sigma_of(step_float):
    remain = 1.0 - step_float / TSTEPS
    return 5.0 * remain / (1.0 + 4.0 * remain)


def remote(src, dst, send_sem, recv_sem, target):
    return pltpu.make_async_remote_copy(
        src_ref=src,
        dst_ref=dst,
        send_sem=send_sem,
        recv_sem=recv_sem,
        device_id=target,
        device_id_type=MESH,
    )


def step_kernel(
    chips,
    latent,
    counts,
    steps,
    gain,
    embed_in,
    modulation_in,
    head_mod_in,
    head_weight_in,
    wqkv,
    wo,
    stale,
    velocity,
    new_latent,
    fresh,
    embed,
    modulation,
    head_mod,
    head_weight,
    table_sem,
    value_sem,
    wbuf,
    kvbuf,
    live_buf,
    meta,
    lat_stage,
    lat_owner,
    lat_home,
    hid,
    proj,
    normed,
    q_buf,
    k_buf,
    v_buf,
    attended,
    h1_stage,
    h1_buf,
    h1_home,
    fresh_stage,
    vel_stage,
    vel_buf,
    w_local,
    wy_send,
    wy_recv,
    ws_send,
    ws_recv,
    wf_send,
    wf_recv,
    zr_send,
    zr_recv,
    zf_send,
    zf_recv,
    kv_send,
    kv_recv,
    kf_send,
    kf_recv,
    meta_send,
    meta_recv,
    lo_send,
    lo_recv,
    lh_send,
    lh_recv,
    h1_send,
    h1_recv,
    hh_send,
    hh_recv,
    vel_send,
    vel_recv,
    out_sem,
):
    s = lax.axis_index("section")
    z = lax.axis_index("patch")
    f = lax.axis_index("fsdp")
    c = lax.rem(f, 2)
    g = f // 2
    model = embed.shape[1]
    shard_rows = wqkv.shape[1]
    slots = kvbuf.shape[2]
    half = slots // 2
    part_cols = model // 2
    tiles = model // TILE
    patches = kvbuf.shape[1]

    def device(section, patch, chip, core):
        return {"section": section, "patch": patch, "fsdp": 2 * chip + core}

    sibling = device(s, z, g, 1 - c)
    tables = [
        pltpu.make_async_copy(src, dst, table_sem.at[i])
        for i, (src, dst) in enumerate(
            [
                (modulation_in, modulation),
                (head_mod_in, head_mod),
                (embed_in, embed),
                (head_weight_in, head_weight),
            ]
        )
    ]
    across = z // 2
    spot = lax.rem(z, 2)

    barrier = pltpu.get_barrier_semaphore()
    greeted = 0
    for ds in range(2):
        for dz in range(patches):
            for dc in range(2):
                if ds or dz or dc:
                    pl.semaphore_signal(
                        barrier,
                        inc=1,
                        device_id=device(
                            lax.rem(s + ds, 2), lax.rem(z + dz, patches), g, lax.rem(c + dc, 2)
                        ),
                        device_id_type=MESH,
                    )
                    greeted += 1
    for dg in range(1, chips):
        pl.semaphore_signal(
            barrier, inc=1, device_id=device(s, z, lax.rem(g + dg, chips), c), device_id_type=MESH
        )
        greeted += 1
    pl.semaphore_wait(barrier, greeted)

    def weight_src(t):
        if t < 3:
            return wqkv.at[0, :, t * model : (t + 1) * model]
        return wo.at[0]

    def weight_rows(t, owner):
        return wbuf.at[t, pl.ds(pl.multiple_of(owner * shard_rows, shard_rows), shard_rows), :]

    def w_own(t):
        return pltpu.make_async_copy(weight_src(t), weight_rows(t, f), w_local.at[t])

    def cols_of(q, start=0):
        return pl.ds(pl.multiple_of(start + q * part_cols, part_cols), part_cols)

    def owner_back(dg):
        return 2 * lax.rem(g + chips - dg, chips) + c

    def w_across(t, dg):
        src, dst = weight_src(t), weight_rows(t, f)
        if t in SHARED:
            src = wo.at[0, :, cols_of(spot)] if t == 3 else wqkv.at[0, :, cols_of(spot, t * model)]
            dst = part_of(t, 0, spot)
        return remote(
            src,
            dst,
            wy_send.at[t, dg],
            wy_recv.at[t, dg],
            device(s, z, lax.rem(g + dg, chips), c),
        )

    def part_of(t, dg, q):
        rows = pl.ds(pl.multiple_of(owner_back(dg) * shard_rows, shard_rows), shard_rows)
        return wbuf.at[t, rows, cols_of(q)]

    def part_forward(t, dg, q):
        part, at = part_of(t, dg, q), SHARED[t]
        return remote(part, part, zf_send.at[at, dg, q], zf_recv.at[at, dg, q], sibling)

    def part_pair(t, dg, q):
        part, at = part_of(t, dg, q), SHARED[t]
        return remote(
            part, part, zr_send.at[at, dg], zr_recv.at[at, dg], device(s, z + 1 - 2 * spot, g, c)
        )

    def parts_first(t):
        for dg in range(1, chips):
            w_across(t, dg).wait_recv()
            part_pair(t, dg, spot).start()
            part_forward(t, dg, spot).start()

    def parts_second(t):
        for dg in range(1, chips):
            part_pair(t, dg, 1 - spot).wait_recv()
            part_forward(t, dg, 1 - spot).start()
        w_own(t).wait()
        w_sibling(t).wait_recv()
        for dg in range(1, chips):
            for q in range(2):
                part_forward(t, dg, q).wait_recv()

    def parts_sent():
        for t in SHARED:
            for dg in range(1, chips):
                part_pair(t, dg, spot).wait_send()
                for q in range(2):
                    part_forward(t, dg, q).wait_send()

    def w_sibling(t):
        return remote(weight_src(t), weight_rows(t, f), ws_send.at[t], ws_recv.at[t], sibling)

    def w_forward(t, dg):
        rows = weight_rows(t, 2 * lax.rem(g + chips - dg, chips) + c)
        return remote(rows, rows, wf_send.at[t, dg], wf_recv.at[t, dg], sibling)

    def kv_src(j, x):
        if x == 1:
            return fresh_stage.at[j, :, model:]
        return stale.at[0, j, 0, :, :model]

    def value_in(j):
        return pltpu.make_async_copy(
            stale.at[0, j, 0, :, model:], fresh_stage.at[j, :, model:], value_sem.at[j]
        )

    def kv_is_self(j, x):
        return jnp.logical_and(2 * c + j == z, c == x)

    def kv_remote(j, x):
        return remote(
            kv_src(j, x),
            kvbuf.at[x, z],
            kv_send.at[j, x],
            kv_recv.at[z],
            device(s, 2 * c + j, g, x),
        )

    def kv_arrival(p):
        return remote(kvbuf.at[c, p], kvbuf.at[c, p], kf_send.at[p], kv_recv.at[p], sibling)

    def kv_forward(p):
        return remote(kvbuf.at[c, p], kvbuf.at[c, p], kf_send.at[p], kf_recv.at[p], sibling)

    def kv_start(j, x):
        @pl.when(kv_is_self(j, x))
        def _():
            pltpu.make_async_copy(kv_src(j, x), kvbuf.at[x, z], kv_recv.at[z]).start()

        @pl.when(jnp.logical_not(kv_is_self(j, x)))
        def _():
            kv_remote(j, x).start()

    def across_start(t):
        for dg in range(1, chips):
            w_across(t, dg).start()

    across_start(1)
    across_start(3)
    kv_start(0, 0)
    kv_start(1, 0)
    for table in tables:
        table.start()
    for j in range(2):
        value_in(j).start()
    for table in tables:
        table.wait()

    for j in range(2):
        step = steps[j]
        video = 2 * c + j
        for part in range(3):
            meta[video, part : part + 1, :] = modulation[
                step, :, part * model : (part + 1) * model
            ]
        for part in range(2):
            meta[video, 3 + part : 4 + part, :] = head_mod[
                pl.ds(step, 1), part * model : (part + 1) * model
            ]
        for p in range(patches):
            meta[video, 5 + p : 6 + p, :] = jnp.full((1, model), counts[j, p].astype(jnp.float32))
        lat_stage[j] = latent[j, 0].astype(jnp.bfloat16)
    mine = meta.at[pl.ds(2 * c, 2)]
    meta_copy = remote(mine, mine, meta_send, meta_recv, sibling)
    meta_copy.start()

    def lat_owner_self(j):
        return jnp.logical_and(s == 0, jnp.logical_and(2 * c + j == z, across == c))

    def lat_owner_copy(j):
        return remote(
            lat_stage.at[j],
            lat_owner.at[spot, :, pl.ds(pl.multiple_of(s * half, half), half)],
            lo_send.at[j],
            lo_recv.at[spot, s],
            device(0, 2 * c + j, g, across),
        )

    def lat_home_copy(j):
        return remote(
            lat_stage.at[j],
            lat_home.at[j, :, pl.ds(pl.multiple_of(s * half, half), half)],
            lh_send.at[j],
            lh_recv.at[j, s],
            device(0, z, g, c),
        )

    for j in range(2):

        @pl.when(lat_owner_self(j))
        def _():
            pltpu.make_async_copy(
                lat_stage.at[j],
                lat_owner.at[spot, :, pl.ds(pl.multiple_of(s * half, half), half)],
                lo_recv.at[spot, s],
            ).start()

        @pl.when(jnp.logical_not(lat_owner_self(j)))
        def _():
            lat_owner_copy(j).start()

        @pl.when(s == 1)
        def _():
            lat_home_copy(j).start()

        @pl.when(s == 0)
        def _():
            pltpu.make_async_copy(
                lat_stage.at[j], lat_home.at[j, :, :half], lh_recv.at[j, 0]
            ).start()

    for t in range(4):
        w_own(t).start()
        w_sibling(t).start()

    meta_copy.wait()

    for p in range(patches):
        row = lax.broadcasted_iota(jnp.int32, (slots, HD), 0).astype(jnp.float32)
        live = row < meta[z, 5 + p : 6 + p, :HD]
        live_buf[p] = jnp.where(live, 1.0, 0.0).astype(jnp.bfloat16)

    def weights_arrive(t):
        for dg in range(1, chips):
            w_across(t, dg).wait_recv()
        if t == 0:
            across_start(2)
        for dg in range(1, chips):
            w_forward(t, dg).start()
        w_own(t).wait()
        w_sibling(t).wait_recv()
        for dg in range(1, chips):
            w_forward(t, dg).wait_recv()

    def in_rows(count, step, body, unroll):
        def one(i, carry):
            body(pl.multiple_of(i * step, step))
            return carry

        lax.fori_loop(0, count // step, one, 0, unroll=unroll)

    def mask_keys(p, key_ref, base):
        first = key_ref[pl.ds(base, 16), :][0:1, :].astype(jnp.float32)
        last_row = meta[z, pl.ds(5 + p, 1), :]

        def rows_of(at):
            rows = pl.ds(base + at, 16)
            row = lax.broadcasted_iota(jnp.int32, (16, model), 0) + at
            live = row.astype(jnp.float32) < last_row
            key_ref[rows, :] = jnp.where(live, key_ref[rows, :].astype(jnp.float32), first).astype(
                jnp.bfloat16
            )

        in_rows(slots, 16, rows_of, 4)

    def mask_values(value_ref, base, live):
        def rows_of(at):
            rows = pl.ds(base + at, 16)
            row = lax.broadcasted_iota(jnp.int32, (16, model), 0) + at
            value_ref[rows, :] = jnp.where(
                row.astype(jnp.float32) < live, value_ref[rows, :].astype(jnp.float32), 0.0
            ).astype(jnp.bfloat16)

        in_rows(slots, 16, rows_of, 4)

    def values_ready():
        for j in range(2):
            value_in(j).wait()
            mask_values(fresh_stage.at[j, :, model:], 0, counts[j, z].astype(jnp.float32))

    def keys_early():
        @pl.when(c == 0)
        def _():
            for p in range(patches):
                kv_arrival(p).wait_recv()
                kv_forward(p).start()
            for p in range(patches):
                kv_forward(p).wait_send()
                mask_keys(p, kvbuf.at[0, p], 0)

    def caches_arrive():
        @pl.when(c == 1)
        def _():
            for p in range(patches):
                kv_forward(p).wait_recv()
                mask_keys(p, kvbuf.at[0, p], 0)
            for p in range(patches):
                kv_arrival(p).wait_recv()
                kv_forward(p).start()
            for p in range(patches):
                kv_forward(p).wait_send()

        @pl.when(c == 0)
        def _():
            for p in range(patches):
                kv_forward(p).wait_recv()

    def kv_sent():
        for j in range(2):
            for x in range(2):

                @pl.when(jnp.logical_not(kv_is_self(j, x)))
                def _():
                    kv_remote(j, x).wait_send()

    def multiply(left, weight, sink):
        def tile(i, carry):
            cols = pl.ds(pl.multiple_of(i * TILE, TILE), TILE)
            sink(i, cols, jnp.dot(left[...], weight[:, cols], preferred_element_type=jnp.float32))
            return carry

        lax.fori_loop(0, tiles, tile, 0)

    def embed_rows(lat_ref, base):
        def tile(i, carry):
            cols = pl.ds(pl.multiple_of(i * TILE, TILE), TILE)
            hid[pl.ds(base, slots), cols] = lax.dot_general(
                lat_ref[...],
                embed[:, cols],
                (((0,), (0,)), ((), ())),
                preferred_element_type=jnp.float32,
            )
            return carry

        lax.fori_loop(0, tiles, tile, 0)

    def norm_block(source, video, shift_row, scale_row, base, at):
        shift = meta[video, shift_row : shift_row + 1, :]
        scale = 1.0 + meta[video, scale_row : scale_row + 1, :]
        values = source[pl.ds(at, 16), :].astype(jnp.float32)
        center = values - jnp.mean(values, axis=-1, keepdims=True)
        unit = center * lax.rsqrt(jnp.mean(center * center, axis=-1, keepdims=True) + EPS)
        normed[pl.ds(base + at, 16), :] = (unit * scale + shift).astype(jnp.bfloat16)

    def norm_rows(source, video, shift_row, scale_row, base):
        def rows_of(at):
            norm_block(source, video, shift_row, scale_row, base, at)

        in_rows(slots, 16, rows_of, 4)

    def rms_block(out_ref, cols, gain_cols, factor, base, at, out_base, live):
        values = proj[pl.ds(base + at, 16), :]
        scaled = values * lax.rsqrt(jnp.mean(values * values, axis=-1, keepdims=True) + EPS)
        scaled = scaled * (gain[:, gain_cols] * factor)
        if live is not None:
            row = lax.broadcasted_iota(jnp.int32, (16, model), 0) + at
            scaled = jnp.where(row < live, scaled, 0.0)
        out_ref[pl.ds(out_base + at, 16), cols] = scaled.astype(jnp.bfloat16)

    def rms_rows(out_ref, cols, gain_cols, factor, base, count, out_base, live=None):
        def rows_of(at):
            rms_block(out_ref, cols, gain_cols, factor, base, at, out_base, live)

        in_rows(count, 16, rows_of, 4)

    def multiply_beside(left, weight, sink, row_work):
        blocks = slots // 16
        done = 0
        for i in range(tiles):
            cols = slice(i * TILE, (i + 1) * TILE)
            product = jnp.dot(left[...], weight[:, cols], preferred_element_type=jnp.float32)
            until = blocks * (i + 1) // tiles
            if row_work is not None:
                for at in range(done, until):
                    row_work(at * 16)
            done = until
            sink(i, cols, product)

    def attend(k, base):
        own = 2 * c + k
        mine = pl.ds(base, slots)

        def head(h, carry):
            cols = pl.ds(pl.multiple_of(h * HD, HD), HD)
            query = q_buf[mine, cols]
            scores = []
            for b in range(patches):
                p = lax.rem(own + b, patches)
                keys = k_buf[mine, cols] if b == 0 else kvbuf[0, p, :, cols]
                scores.append(
                    lax.dot_general(
                        query, keys, (((1,), (1,)), ((), ())), preferred_element_type=jnp.float32
                    )
                )
            top = scores[0]
            for score in scores[1:]:
                top = jnp.maximum(top, score)
            top = jnp.max(top, axis=1, keepdims=True)
            mixed = None
            for b in range(patches):
                p = lax.rem(own + b, patches)
                weight = jnp.exp2(scores[b] - top).astype(jnp.bfloat16)
                values = v_buf[mine, cols] if b == 0 else kvbuf[1, p, :, cols]
                both = jnp.concatenate([values, live_buf[p]], axis=1)
                part = jnp.dot(weight, both, preferred_element_type=jnp.float32)
                mixed = part if mixed is None else mixed + part
            attended[:, cols] = (mixed[:, :HD] / mixed[:, HD:]).astype(jnp.bfloat16)
            return carry

        lax.fori_loop(0, HEADS, head, 0, unroll=4)

    def home_of(k, section):
        return device(section, 2 * c + k, g, across)

    def home_is_self(k):
        return jnp.logical_and(2 * c + k == z, across == c)

    def h1_tile(ref, i):
        return ref.at[:, pl.ds(pl.multiple_of(i * TILE, TILE), TILE)]

    def h1_over(k, i):
        return remote(
            h1_tile(h1_stage.at[k], i),
            h1_tile(h1_buf.at[k], i),
            h1_send.at[k, i],
            h1_recv.at[k, i],
            device(1, z, g, c),
        )

    def h1_to_home(k, i):
        return remote(
            h1_tile(h1_buf.at[k], i),
            h1_tile(h1_home.at[spot], i),
            hh_send.at[k, i],
            hh_recv.at[spot, i],
            home_of(k, 1),
        )

    def h1_arrives(k, i):
        h1_over(k, i).wait_recv()

        @pl.when(home_is_self(k))
        def _():
            pltpu.make_async_copy(
                h1_tile(h1_buf.at[k], i), h1_tile(h1_home.at[spot], i), hh_recv.at[spot, i]
            ).start()

        @pl.when(jnp.logical_not(home_is_self(k)))
        def _():
            h1_to_home(k, i).start()

    def vel_src(k, section):
        return vel_stage.at[k, :, section * half : (section + 1) * half]

    def vel_to_home(k, section):
        return remote(
            vel_src(k, section),
            vel_buf.at[spot],
            vel_send.at[k, section],
            vel_recv.at[spot],
            home_of(k, section),
        )

    factor = math.log2(math.e) / math.sqrt(HD)

    def project(t, base, count):
        rows = pl.ds(base, count)

        def sink_proj(i, cols, product):
            proj[rows, cols] = product

        def sink_value(i, cols, product):
            v_buf[rows, cols] = product.astype(jnp.bfloat16)

        multiply(normed.at[rows], wbuf.at[t], sink_value if t == 2 else sink_proj)
        if t == 0:
            rms_rows(q_buf, slice(None), slice(0, model), factor, base, count, base)
        if t == 1:
            rms_rows(k_buf, slice(None), slice(model, 2 * model), 1.0, base, count, base)

    def update(k, base, after):
        rows = pl.ds(base, slots)

        def sink_update(i, cols, product):
            after(i, cols, hid[rows, cols] + meta[z, 2:3, cols] * product)

        multiply(attended, wbuf.at[3], sink_update)

    def fresh_out(j):
        return pltpu.make_async_copy(fresh_stage.at[j], fresh.at[0, j, 0], out_sem.at[j])

    def sink_fresh_of(j):
        live = counts[j, z]

        def sink_fresh(i, cols, product):
            row = lax.broadcasted_iota(jnp.int32, product.shape, 0)
            fresh_stage[j, :, pl.ds(pl.multiple_of(model + i * TILE, TILE), TILE)] = jnp.where(
                row < live, product, 0.0
            ).astype(jnp.bfloat16)

        return sink_fresh

    def sink_low(i, cols, product):
        proj[pl.ds(0, slots), cols] = product

    def home(j):
        norm_rows(hid.at[pl.ds(0, slots)], 2 * c + j, 0, 1, 0)
        first = normed.at[pl.ds(0, slots)]
        multiply(first, wbuf.at[1], sink_low)
        rms_rows(
            fresh_stage.at[j],
            slice(0, model),
            slice(model, 2 * model),
            1.0,
            0,
            slots,
            0,
            counts[j, z],
        )
        multiply(first, wbuf.at[2], sink_fresh_of(j))
        fresh_out(j).start()

    def first_parts():
        parts_first(1)
        parts_first(3)
        across_start(0)
        kv_start(0, 1)
        kv_start(1, 1)

    @pl.when(s == 0)
    def _():
        def enter(k, carry):
            for part in range(2):
                cols = pl.ds(part * half, half)
                remote(
                    lat_owner.at[k, :, cols],
                    lat_owner.at[k, :, cols],
                    lo_send.at[0],
                    lo_recv.at[k, part],
                    sibling,
                ).wait_recv()
            base = pl.multiple_of(k * slots, slots)
            embed_rows(lat_owner.at[k], base)
            norm_rows(hid.at[pl.ds(base, slots)], z, 0, 1, base)
            return carry

        values_ready()
        first_parts()
        lax.fori_loop(0, 2, enter, 0)
        weights_arrive(0)
        project(0, 0, 2 * slots)
        keys_early()
        parts_second(1)
        project(1, 0, 2 * slots)
        parts_second(3)
        caches_arrive()
        weights_arrive(2)

        def leave(turn, carry):
            k = lax.rem(turn + z, 2)
            base = pl.multiple_of(k * slots, slots)
            project(2, base, slots)
            mask_keys(2 * c + k, k_buf, base)
            mask_values(v_buf, base, meta[z, pl.ds(5 + 2 * c + k, 1), :])
            attend(k, base)

            def after(i, cols, hidden):
                h1_stage[k, :, cols] = hidden.astype(jnp.bfloat16)
                h1_over(k, i).start()

            update(k, base, after)
            return carry

        lax.fori_loop(0, 2, leave, 0)

        def home_first(j, carry):
            for part in range(2):
                cols = pl.ds(part * half, half)
                remote(
                    lat_home.at[j, :, cols],
                    lat_home.at[j, :, cols],
                    lh_send.at[0],
                    lh_recv.at[j, part],
                    sibling,
                ).wait_recv()
            embed_rows(lat_home.at[j], 0)
            home(j)
            return carry

        kv_sent()
        lax.fori_loop(0, 2, home_first, 0)
        for k in range(2):
            for i in range(tiles):
                h1_over(k, i).wait_send()

    @pl.when(s == 1)
    def _():
        values_ready()
        first_parts()
        weights_arrive(0)
        keys_early()
        parts_second(1)
        parts_second(3)
        caches_arrive()
        weights_arrive(2)

        def turn_of(turn, carry):
            k = lax.rem(turn + z, 2)
            base = pl.multiple_of(k * slots, slots)
            rows = pl.ds(base, slots)

            @pl.when(turn == 0)
            def _():
                for i in range(tiles):
                    h1_arrives(k, i)

            @pl.when(turn == 1)
            def _():
                h1_arrives(k, tiles - 1)

            other = pl.multiple_of(slots - base, slots)
            here, there = normed.at[rows], normed.at[pl.ds(other, slots)]
            j = lax.rem(turn + z, 2)
            norm_rows(h1_buf.at[k], z, 0, 1, base)

            def sink_high(i, cols, product):
                proj[pl.ds(slots, slots), cols] = product

            def sink_value(i, cols, product):
                v_buf[rows, cols] = product.astype(jnp.bfloat16)

            def query_rows(at):
                rms_block(q_buf, slice(None), slice(0, model), factor, 0, at, base, None)

            def key_rows(at):
                rms_block(
                    k_buf, slice(None), slice(model, 2 * model), 1.0, slots, at, base, None
                )

            def home_rows(at):
                norm_block(h1_home.at[j], 2 * c + j, 0, 1, other, at)

            def fresh_rows(at):
                rms_block(
                    fresh_stage.at[j],
                    slice(0, model),
                    slice(model, 2 * model),
                    1.0,
                    0,
                    at,
                    0,
                    counts[j, z],
                )

            def sink_update(i, cols, product):
                hid[rows, cols] = (
                    h1_buf[k, :, cols].astype(jnp.float32) + meta[z, 2:3, cols] * product
                )

            multiply_beside(here, wbuf.at[0], sink_low, None)
            multiply_beside(here, wbuf.at[1], sink_high, query_rows)
            multiply_beside(here, wbuf.at[2], sink_value, key_rows)

            @pl.when(turn == 0)
            def _():
                h1_arrives(1 - k, 0)

            mask_keys(2 * c + k, k_buf, base)
            mask_values(v_buf, base, meta[z, pl.ds(5 + 2 * c + k, 1), :])
            attend(k, base)

            @pl.when(turn == 0)
            def _():
                h1_arrives(1 - k, 1)

            for i in range(tiles):
                remote(
                    h1_tile(h1_home.at[j], i),
                    h1_tile(h1_home.at[j], i),
                    hh_send.at[0, i],
                    hh_recv.at[j, i],
                    sibling,
                ).wait_recv()
            multiply_beside(attended, wbuf.at[3], sink_update, home_rows)
            norm_rows(hid.at[rows], z, 3, 4, base)
            vel_stage[k] = lax.dot_general(
                head_weight[...],
                normed[rows, :],
                (((1,), (1,)), ((), ())),
                preferred_element_type=jnp.float32,
            )
            vel_to_home(k, 0).start()

            @pl.when(home_is_self(k))
            def _():
                pltpu.make_async_copy(vel_src(k, 1), vel_buf.at[spot], vel_recv.at[spot]).start()

            @pl.when(jnp.logical_not(home_is_self(k)))
            def _():
                vel_to_home(k, 1).start()

            multiply_beside(there, wbuf.at[1], sink_low, None)
            multiply_beside(there, wbuf.at[2], sink_fresh_of(j), fresh_rows)
            fresh_out(j).start()
            return carry

        kv_sent()
        lax.fori_loop(0, 2, turn_of, 0)
        for k in range(2):
            vel_to_home(k, 0).wait_send()

            @pl.when(jnp.logical_not(home_is_self(k)))
            def _():
                for i in range(tiles):
                    h1_to_home(k, i).wait_send()
                vel_to_home(k, 1).wait_send()

    for t in range(4):
        for dg in range(1, chips):
            w_across(t, dg).wait_send()
            if t not in SHARED:
                w_forward(t, dg).wait_send()
        w_sibling(t).wait_send()
    parts_sent()
    for j in range(2):

        @pl.when(jnp.logical_not(lat_owner_self(j)))
        def _():
            lat_owner_copy(j).wait_send()

        @pl.when(s == 1)
        def _():
            lat_home_copy(j).wait_send()

    for j in range(2):
        remote(
            vel_buf.at[j], vel_buf.at[j], vel_send.at[0, 0], vel_recv.at[j], sibling
        ).wait_recv()
        slot = lax.broadcasted_iota(jnp.int32, vel_buf.shape[1:], 1) + s * half
        step = jnp.full(vel_buf.shape[1:], steps[j].astype(jnp.float32))
        value = jnp.where(slot < counts[j, z], vel_buf[j], 0.0)
        velocity[j, 0] = value
        new_latent[j, 0] = latent[j, 0] + (sigma_of(step + 1.0) - sigma_of(step)) * value
        fresh_out(j).wait()


def hand_on(velocity_in, latent_in, fresh_in, velocity, new_latent, fresh):
    velocity[...] = velocity_in[...]
    new_latent[...] = latent_in[...]
    fresh[...] = fresh_in[...]


def body(
    chips,
    latent,
    counts,
    steps_idx,
    embed_weight,
    wqkv,
    wo,
    qk_gain,
    modulation,
    head_mod,
    head_weight,
    stale_cache,
):
    videos, _, half, channels = latent.shape
    patches = counts.shape[1]
    slots = stale_cache.shape[3]
    model = embed_weight.shape[1]
    assert videos == 2 and patches == 4
    bf16, f32 = jnp.bfloat16, jnp.float32
    vmem = pl.BlockSpec(memory_space=pltpu.VMEM)
    smem = pl.BlockSpec(memory_space=pltpu.SMEM)
    anywhere = pl.BlockSpec(memory_space=pl.ANY)
    dma = pltpu.SemaphoreType.DMA
    latent = jnp.swapaxes(latent, 2, 3)
    velocity, new_latent, fresh = pl.pallas_call(
        functools.partial(step_kernel, chips),
        in_specs=[vmem, smem, smem, vmem] + [anywhere] * 7,
        out_specs=[vmem, vmem, anywhere],
        out_shape=[
            jax.ShapeDtypeStruct(latent.shape, f32),
            jax.ShapeDtypeStruct(latent.shape, f32),
            jax.ShapeDtypeStruct(stale_cache.shape, bf16),
        ],
        scratch_shapes=[
            pltpu.VMEM(embed_weight.shape, bf16),
            pltpu.VMEM((modulation.shape[1], 1, 3 * model), f32),
            pltpu.VMEM(head_mod.shape, f32),
            pltpu.VMEM((channels, model), bf16),
            dma((4,)),
            dma((2,)),
            pltpu.VMEM((4, model, model), bf16),
            pltpu.VMEM((2, patches, slots, model), bf16),
            pltpu.VMEM((patches, slots, HD), bf16),
            pltpu.VMEM((4, META_ROWS, model), f32),
            pltpu.VMEM((2, channels, half), bf16),
            pltpu.VMEM((2, channels, slots), bf16),
            pltpu.VMEM((2, channels, slots), bf16),
            pltpu.VMEM((2 * slots, model), f32),
            pltpu.VMEM((2 * slots, model), f32),
            pltpu.VMEM((2 * slots, model), bf16),
            pltpu.VMEM((2 * slots, model), bf16),
            pltpu.VMEM((2 * slots, model), bf16),
            pltpu.VMEM((2 * slots, model), bf16),
            pltpu.VMEM((slots, model), bf16),
            pltpu.VMEM((2, slots, model), bf16),
            pltpu.VMEM((2, slots, model), bf16),
            pltpu.VMEM((2, slots, model), bf16),
            pltpu.VMEM((2, slots, 2 * model), bf16),
            pltpu.VMEM((2, channels, slots), f32),
            pltpu.VMEM((2, channels, half), f32),
            dma((4,)),
            dma((4, chips)),
            dma((4, chips)),
            dma((4,)),
            dma((4,)),
            dma((3, chips)),
            dma((3, chips)),
            dma((2, chips)),
            dma((2, chips)),
            dma((2, chips, 2)),
            dma((2, chips, 2)),
            dma((2, 2)),
            dma((patches,)),
            dma((patches,)),
            dma((patches,)),
            dma,
            dma,
            dma((2,)),
            dma((2, 2)),
            dma((2,)),
            dma((2, 2)),
            dma((2, model // TILE)),
            dma((2, model // TILE)),
            dma((2, model // TILE)),
            dma((2, model // TILE)),
            dma((2, 2)),
            dma((2,)),
            dma((2,)),
        ],
        compiler_params=pltpu.CompilerParams(
            collective_id=0, has_side_effects=True, vmem_limit_bytes=58 * 1024 * 1024
        ),
    )(
        latent,
        counts,
        steps_idx,
        qk_gain,
        embed_weight,
        jnp.swapaxes(modulation, 0, 1),
        head_mod,
        head_weight.T,
        wqkv,
        wo,
        stale_cache,
    )
    small = pl.BlockSpec(velocity.shape, lambda i: (0, 0, 0, 0))
    large = pl.BlockSpec((1, 1, 1, slots // 2, 2 * model), lambda i: (0, i // 2, 0, i % 2, 0))
    velocity, new_latent, fresh = pl.pallas_call(
        hand_on,
        grid=(4,),
        in_specs=[small, small, large],
        out_specs=[small, small, large],
        out_shape=[jax.ShapeDtypeStruct(a.shape, a.dtype) for a in (velocity, new_latent, fresh)],
    )(velocity, new_latent, fresh)
    return jnp.swapaxes(velocity, 2, 3), jnp.swapaxes(new_latent, 2, 3), fresh


def solution(mesh):
    chips = mesh.shape["fsdp"] // 2
    in_specs = (
        P("fsdp", "patch", "section", None),
        P("fsdp", None),
        P("fsdp"),
        P(),
        P("section", "fsdp", None),
        P("section", "fsdp", None),
        P("section", None),
        P("section", None, None),
        P(),
        P(),
        P("section", "fsdp", "patch", None, None),
    )
    out_specs = (
        P("fsdp", "patch", "section", None),
        P("fsdp", "patch", "section", None),
        P("section", "fsdp", "patch", None, None),
    )
    return jax.shard_map(
        functools.partial(body, chips),
        mesh=mesh,
        in_specs=in_specs,
        out_specs=out_specs,
        check_vma=False,
    )
```

```python
import functools
import math

import jax
import jax.numpy as jnp
from jax import lax
from jax.experimental import pallas as pl
from jax.experimental.pallas import tpu as pltpu
from jax.sharding import PartitionSpec as P

HEADS = 12
HD = 128
TSTEPS = 50
EPS = 1e-06
MESH = pl.DeviceIdType.MESH
TILE = 512
META_ROWS = 16
SHARED = {1: 0, 3: 1}


def sigma_of(step_float):
    remain = 1.0 - step_float / TSTEPS
    return 5.0 * remain / (1.0 + 4.0 * remain)


def remote(src, dst, send_sem, recv_sem, target):
    return pltpu.make_async_remote_copy(
        src_ref=src,
        dst_ref=dst,
        send_sem=send_sem,
        recv_sem=recv_sem,
        device_id=target,
        device_id_type=MESH,
    )


def step_kernel(
    chips,
    latent,
    counts,
    steps,
    gain,
    embed_in,
    modulation_in,
    head_mod_in,
    head_weight_in,
    wqkv,
    wo,
    stale,
    velocity,
    new_latent,
    fresh,
    embed,
    modulation,
    head_mod,
    head_weight,
    table_sem,
    value_sem,
    wbuf,
    kvbuf,
    live_buf,
    meta,
    lat_stage,
    lat_owner,
    lat_home,
    hid,
    proj,
    normed,
    q_buf,
    k_buf,
    v_buf,
    attended,
    h1_stage,
    h1_buf,
    h1_home,
    fresh_stage,
    vel_stage,
    vel_buf,
    w_local,
    wy_send,
    wy_recv,
    ws_send,
    ws_recv,
    wf_send,
    wf_recv,
    zr_send,
    zr_recv,
    zf_send,
    zf_recv,
    kv_send,
    kv_recv,
    kf_send,
    kf_recv,
    meta_send,
    meta_recv,
    lo_send,
    lo_recv,
    lh_send,
    lh_recv,
    h1_send,
    h1_recv,
    hh_send,
    hh_recv,
    vel_send,
    vel_recv,
    out_sem,
):
    s = lax.axis_index("section")
    z = lax.axis_index("patch")
    f = lax.axis_index("fsdp")
    c = lax.rem(f, 2)
    g = f // 2
    model = embed.shape[1]
    shard_rows = wqkv.shape[1]
    slots = kvbuf.shape[2]
    half = slots // 2
    part_cols = model // 2
    tiles = model // TILE
    patches = kvbuf.shape[1]

    def device(section, patch, chip, core):
        return {"section": section, "patch": patch, "fsdp": 2 * chip + core}

    sibling = device(s, z, g, 1 - c)
    tables = [
        pltpu.make_async_copy(src, dst, table_sem.at[i])
        for i, (src, dst) in enumerate(
            [
                (modulation_in, modulation),
                (head_mod_in, head_mod),
                (embed_in, embed),
                (head_weight_in, head_weight),
            ]
        )
    ]
    across = z // 2
    spot = lax.rem(z, 2)

    barrier = pltpu.get_barrier_semaphore()
    greeted = 0
    for ds in range(2):
        for dz in range(patches):
            for dc in range(2):
                if ds or dz or dc:
                    pl.semaphore_signal(
                        barrier,
                        inc=1,
                        device_id=device(
                            lax.rem(s + ds, 2), lax.rem(z + dz, patches), g, lax.rem(c + dc, 2)
                        ),
                        device_id_type=MESH,
                    )
                    greeted += 1
    for dg in range(1, chips):
        pl.semaphore_signal(
            barrier, inc=1, device_id=device(s, z, lax.rem(g + dg, chips), c), device_id_type=MESH
        )
        greeted += 1
    pl.semaphore_wait(barrier, greeted)

    def weight_src(t):
        if t < 3:
            return wqkv.at[0, :, t * model : (t + 1) * model]
        return wo.at[0]

    def weight_rows(t, owner):
        return wbuf.at[t, pl.ds(pl.multiple_of(owner * shard_rows, shard_rows), shard_rows), :]

    def w_own(t):
        return pltpu.make_async_copy(weight_src(t), weight_rows(t, f), w_local.at[t])

    def cols_of(q, start=0):
        return pl.ds(pl.multiple_of(start + q * part_cols, part_cols), part_cols)

    def owner_back(dg):
        return 2 * lax.rem(g + chips - dg, chips) + c

    def w_across(t, dg):
        src, dst = weight_src(t), weight_rows(t, f)
        if t in SHARED:
            src = wo.at[0, :, cols_of(spot)] if t == 3 else wqkv.at[0, :, cols_of(spot, t * model)]
            dst = part_of(t, 0, spot)
        return remote(
            src,
            dst,
            wy_send.at[t, dg],
            wy_recv.at[t, dg],
            device(s, z, lax.rem(g + dg, chips), c),
        )

    def part_of(t, dg, q):
        rows = pl.ds(pl.multiple_of(owner_back(dg) * shard_rows, shard_rows), shard_rows)
        return wbuf.at[t, rows, cols_of(q)]

    def part_forward(t, dg, q):
        part, at = part_of(t, dg, q), SHARED[t]
        return remote(part, part, zf_send.at[at, dg, q], zf_recv.at[at, dg, q], sibling)

    def part_pair(t, dg, q):
        part, at = part_of(t, dg, q), SHARED[t]
        return remote(
            part, part, zr_send.at[at, dg], zr_recv.at[at, dg], device(s, z + 1 - 2 * spot, g, c)
        )

    def parts_first(t):
        for dg in range(1, chips):
            w_across(t, dg).wait_recv()
            part_pair(t, dg, spot).start()
            part_forward(t, dg, spot).start()

    def parts_second(t):
        for dg in range(1, chips):
            part_pair(t, dg, 1 - spot).wait_recv()
            part_forward(t, dg, 1 - spot).start()
        w_own(t).wait()
        w_sibling(t).wait_recv()
        for dg in range(1, chips):
            for q in range(2):
                part_forward(t, dg, q).wait_recv()

    def parts_sent():
        for t in SHARED:
            for dg in range(1, chips):
                part_pair(t, dg, spot).wait_send()
                for q in range(2):
                    part_forward(t, dg, q).wait_send()

    def w_sibling(t):
        return remote(weight_src(t), weight_rows(t, f), ws_send.at[t], ws_recv.at[t], sibling)

    def w_forward(t, dg):
        rows = weight_rows(t, 2 * lax.rem(g + chips - dg, chips) + c)
        return remote(rows, rows, wf_send.at[t, dg], wf_recv.at[t, dg], sibling)

    def kv_src(j, x):
        if x == 1:
            return fresh_stage.at[j, :, model:]
        return stale.at[0, j, 0, :, :model]

    def value_in(j):
        return pltpu.make_async_copy(
            stale.at[0, j, 0, :, model:], fresh_stage.at[j, :, model:], value_sem.at[j]
        )

    def kv_is_self(j, x):
        return jnp.logical_and(2 * c + j == z, c == x)

    def kv_remote(j, x):
        return remote(
            kv_src(j, x),
            kvbuf.at[x, z],
            kv_send.at[j, x],
            kv_recv.at[z],
            device(s, 2 * c + j, g, x),
        )

    def kv_arrival(p):
        return remote(kvbuf.at[c, p], kvbuf.at[c, p], kf_send.at[p], kv_recv.at[p], sibling)

    def kv_forward(p):
        return remote(kvbuf.at[c, p], kvbuf.at[c, p], kf_send.at[p], kf_recv.at[p], sibling)

    def kv_start(j, x):
        @pl.when(kv_is_self(j, x))
        def _():
            pltpu.make_async_copy(kv_src(j, x), kvbuf.at[x, z], kv_recv.at[z]).start()

        @pl.when(jnp.logical_not(kv_is_self(j, x)))
        def _():
            kv_remote(j, x).start()

    def across_start(t):
        for dg in range(1, chips):
            w_across(t, dg).start()

    across_start(1)
    across_start(3)
    across_start(0)
    kv_start(0, 0)
    kv_start(1, 0)
    for table in tables:
        table.start()
    for j in range(2):
        value_in(j).start()
    for table in tables:
        table.wait()

    for j in range(2):
        step = steps[j]
        video = 2 * c + j
        for part in range(3):
            meta[video, part : part + 1, :] = modulation[
                step, :, part * model : (part + 1) * model
            ]
        for part in range(2):
            meta[video, 3 + part : 4 + part, :] = head_mod[
                pl.ds(step, 1), part * model : (part + 1) * model
            ]
        for p in range(patches):
            meta[video, 5 + p : 6 + p, :] = jnp.full((1, model), counts[j, p].astype(jnp.float32))
        lat_stage[j] = latent[j, 0].astype(jnp.bfloat16)
    mine = meta.at[pl.ds(2 * c, 2)]
    meta_copy = remote(mine, mine, meta_send, meta_recv, sibling)
    meta_copy.start()

    def lat_owner_self(j):
        return jnp.logical_and(s == 0, jnp.logical_and(2 * c + j == z, across == c))

    def lat_owner_copy(j):
        return remote(
            lat_stage.at[j],
            lat_owner.at[spot, :, pl.ds(pl.multiple_of(s * half, half), half)],
            lo_send.at[j],
            lo_recv.at[spot, s],
            device(0, 2 * c + j, g, across),
        )

    def lat_home_copy(j):
        return remote(
            lat_stage.at[j],
            lat_home.at[j, :, pl.ds(pl.multiple_of(s * half, half), half)],
            lh_send.at[j],
            lh_recv.at[j, s],
            device(0, z, g, c),
        )

    for j in range(2):

        @pl.when(lat_owner_self(j))
        def _():
            pltpu.make_async_copy(
                lat_stage.at[j],
                lat_owner.at[spot, :, pl.ds(pl.multiple_of(s * half, half), half)],
                lo_recv.at[spot, s],
            ).start()

        @pl.when(jnp.logical_not(lat_owner_self(j)))
        def _():
            lat_owner_copy(j).start()

        @pl.when(s == 1)
        def _():
            lat_home_copy(j).start()

        @pl.when(s == 0)
        def _():
            pltpu.make_async_copy(
                lat_stage.at[j], lat_home.at[j, :, :half], lh_recv.at[j, 0]
            ).start()

    for t in range(4):
        w_own(t).start()
        w_sibling(t).start()

    meta_copy.wait()

    for p in range(patches):
        row = lax.broadcasted_iota(jnp.int32, (slots, HD), 0).astype(jnp.float32)
        live = row < meta[z, 5 + p : 6 + p, :HD]
        live_buf[p] = jnp.where(live, 1.0, 0.0).astype(jnp.bfloat16)

    def weights_arrive(t):
        for dg in range(1, chips):
            w_across(t, dg).wait_recv()
        for dg in range(1, chips):
            w_forward(t, dg).start()
        w_own(t).wait()
        w_sibling(t).wait_recv()
        for dg in range(1, chips):
            w_forward(t, dg).wait_recv()

    def in_rows(count, step, body, unroll):
        def one(i, carry):
            body(pl.multiple_of(i * step, step))
            return carry

        lax.fori_loop(0, count // step, one, 0, unroll=unroll)

    def mask_keys(p, key_ref, base):
        first = key_ref[pl.ds(base, 16), :][0:1, :].astype(jnp.float32)
        last_row = meta[z, pl.ds(5 + p, 1), :]

        def rows_of(at):
            rows = pl.ds(base + at, 16)
            row = lax.broadcasted_iota(jnp.int32, (16, model), 0) + at
            live = row.astype(jnp.float32) < last_row
            key_ref[rows, :] = jnp.where(live, key_ref[rows, :].astype(jnp.float32), first).astype(
                jnp.bfloat16
            )

        in_rows(slots, 16, rows_of, 4)

    def mask_values(value_ref, base, live):
        def rows_of(at):
            rows = pl.ds(base + at, 16)
            row = lax.broadcasted_iota(jnp.int32, (16, model), 0) + at
            value_ref[rows, :] = jnp.where(
                row.astype(jnp.float32) < live, value_ref[rows, :].astype(jnp.float32), 0.0
            ).astype(jnp.bfloat16)

        in_rows(slots, 16, rows_of, 4)

    def values_ready():
        for j in range(2):
            value_in(j).wait()
            mask_values(fresh_stage.at[j, :, model:], 0, counts[j, z].astype(jnp.float32))

    def keys_early():
        @pl.when(c == 0)
        def _():
            for p in range(patches):
                kv_arrival(p).wait_recv()
                kv_forward(p).start()
            for p in range(patches):
                kv_forward(p).wait_send()
                mask_keys(p, kvbuf.at[0, p], 0)

    def caches_arrive():
        @pl.when(c == 1)
        def _():
            for p in range(patches):
                kv_forward(p).wait_recv()
                mask_keys(p, kvbuf.at[0, p], 0)
            for p in range(patches):
                kv_arrival(p).wait_recv()
                kv_forward(p).start()
            for p in range(patches):
                kv_forward(p).wait_send()

        @pl.when(c == 0)
        def _():
            for p in range(patches):
                kv_forward(p).wait_recv()

    def kv_sent():
        for j in range(2):
            for x in range(2):

                @pl.when(jnp.logical_not(kv_is_self(j, x)))
                def _():
                    kv_remote(j, x).wait_send()

    def multiply(left, weight, sink):
        def tile(i, carry):
            cols = pl.ds(pl.multiple_of(i * TILE, TILE), TILE)
            sink(i, cols, jnp.dot(left[...], weight[:, cols], preferred_element_type=jnp.float32))
            return carry

        lax.fori_loop(0, tiles, tile, 0)

    def embed_rows(lat_ref, base):
        def tile(i, carry):
            cols = pl.ds(pl.multiple_of(i * TILE, TILE), TILE)
            hid[pl.ds(base, slots), cols] = lax.dot_general(
                lat_ref[...],
                embed[:, cols],
                (((0,), (0,)), ((), ())),
                preferred_element_type=jnp.float32,
            )
            return carry

        lax.fori_loop(0, tiles, tile, 0)

    def norm_block(source, video, shift_row, scale_row, base, at):
        shift = meta[video, shift_row : shift_row + 1, :]
        scale = 1.0 + meta[video, scale_row : scale_row + 1, :]
        values = source[pl.ds(at, 16), :].astype(jnp.float32)
        center = values - jnp.mean(values, axis=-1, keepdims=True)
        unit = center * lax.rsqrt(jnp.mean(center * center, axis=-1, keepdims=True) + EPS)
        normed[pl.ds(base + at, 16), :] = (unit * scale + shift).astype(jnp.bfloat16)

    def norm_rows(source, video, shift_row, scale_row, base):
        def rows_of(at):
            norm_block(source, video, shift_row, scale_row, base, at)

        in_rows(slots, 16, rows_of, 4)

    def rms_block(out_ref, cols, gain_cols, factor, base, at, out_base, live):
        values = proj[pl.ds(base + at, 16), :]
        scaled = values * lax.rsqrt(jnp.mean(values * values, axis=-1, keepdims=True) + EPS)
        scaled = scaled * (gain[:, gain_cols] * factor)
        if live is not None:
            row = lax.broadcasted_iota(jnp.int32, (16, model), 0) + at
            scaled = jnp.where(row < live, scaled, 0.0)
        out_ref[pl.ds(out_base + at, 16), cols] = scaled.astype(jnp.bfloat16)

    def rms_rows(out_ref, cols, gain_cols, factor, base, count, out_base, live=None):
        def rows_of(at):
            rms_block(out_ref, cols, gain_cols, factor, base, at, out_base, live)

        in_rows(count, 16, rows_of, 4)

    def multiply_beside(left, weight, sink, row_work):
        blocks = slots // 16
        done = 0
        for i in range(tiles):
            cols = slice(i * TILE, (i + 1) * TILE)
            product = jnp.dot(left[...], weight[:, cols], preferred_element_type=jnp.float32)
            until = blocks * (i + 1) // tiles
            if row_work is not None:
                for at in range(done, until):
                    row_work(at * 16)
            done = until
            sink(i, cols, product)

    def attend(k, base):
        own = 2 * c + k
        mine = pl.ds(base, slots)

        def head(h, carry):
            cols = pl.ds(pl.multiple_of(h * HD, HD), HD)
            query = q_buf[mine, cols]
            scores = []
            for b in range(patches):
                p = lax.rem(own + b, patches)
                keys = k_buf[mine, cols] if b == 0 else kvbuf[0, p, :, cols]
                scores.append(
                    lax.dot_general(
                        query, keys, (((1,), (1,)), ((), ())), preferred_element_type=jnp.float32
                    )
                )
            top = scores[0]
            for score in scores[1:]:
                top = jnp.maximum(top, score)
            top = jnp.max(top, axis=1, keepdims=True)
            mixed = None
            for b in range(patches):
                p = lax.rem(own + b, patches)
                weight = jnp.exp2(scores[b] - top).astype(jnp.bfloat16)
                values = v_buf[mine, cols] if b == 0 else kvbuf[1, p, :, cols]
                both = jnp.concatenate([values, live_buf[p]], axis=1)
                part = jnp.dot(weight, both, preferred_element_type=jnp.float32)
                mixed = part if mixed is None else mixed + part
            attended[:, cols] = (mixed[:, :HD] / mixed[:, HD:]).astype(jnp.bfloat16)
            return carry

        lax.fori_loop(0, HEADS, head, 0, unroll=4)

    def home_of(k, section):
        return device(section, 2 * c + k, g, across)

    def home_is_self(k):
        return jnp.logical_and(2 * c + k == z, across == c)

    def h1_tile(ref, i):
        return ref.at[:, pl.ds(pl.multiple_of(i * TILE, TILE), TILE)]

    def h1_over(k, i):
        return remote(
            h1_tile(h1_stage.at[k], i),
            h1_tile(h1_buf.at[k], i),
            h1_send.at[k, i],
            h1_recv.at[k, i],
            device(1, z, g, c),
        )

    def h1_to_home(k, i):
        return remote(
            h1_tile(h1_buf.at[k], i),
            h1_tile(h1_home.at[spot], i),
            hh_send.at[k, i],
            hh_recv.at[spot, i],
            home_of(k, 1),
        )

    def h1_arrives(k, i):
        h1_over(k, i).wait_recv()

        @pl.when(home_is_self(k))
        def _():
            pltpu.make_async_copy(
                h1_tile(h1_buf.at[k], i), h1_tile(h1_home.at[spot], i), hh_recv.at[spot, i]
            ).start()

        @pl.when(jnp.logical_not(home_is_self(k)))
        def _():
            h1_to_home(k, i).start()

    def vel_src(k, section):
        return vel_stage.at[k, :, section * half : (section + 1) * half]

    def vel_to_home(k, section):
        return remote(
            vel_src(k, section),
            vel_buf.at[spot],
            vel_send.at[k, section],
            vel_recv.at[spot],
            home_of(k, section),
        )

    factor = math.log2(math.e) / math.sqrt(HD)

    def project(t, base, count):
        rows = pl.ds(base, count)

        def sink_proj(i, cols, product):
            proj[rows, cols] = product

        multiply(normed.at[rows], wbuf.at[t], sink_proj)
        if t == 0:
            rms_rows(q_buf, slice(None), slice(0, model), factor, base, count, base)
        else:
            rms_rows(k_buf, slice(None), slice(model, 2 * model), 1.0, base, count, base)

    def sink_value_of(k, base):
        last_row = meta[z, pl.ds(5 + 2 * c + k, 1), :TILE]

        def sink_value(i, cols, product):
            row = lax.broadcasted_iota(jnp.int32, product.shape, 0).astype(jnp.float32)
            v_buf[pl.ds(base, slots), cols] = jnp.where(row < last_row, product, 0.0).astype(
                jnp.bfloat16
            )

        return sink_value

    def update(k, base, after):
        rows = pl.ds(base, slots)

        def sink_update(i, cols, product):
            after(i, cols, hid[rows, cols] + meta[z, 2:3, cols] * product)

        multiply(attended, wbuf.at[3], sink_update)

    def fresh_out(j):
        return pltpu.make_async_copy(fresh_stage.at[j], fresh.at[0, j, 0], out_sem.at[j])

    def sink_fresh_of(j):
        live = counts[j, z]

        def sink_fresh(i, cols, product):
            row = lax.broadcasted_iota(jnp.int32, product.shape, 0)
            fresh_stage[j, :, pl.ds(pl.multiple_of(model + i * TILE, TILE), TILE)] = jnp.where(
                row < live, product, 0.0
            ).astype(jnp.bfloat16)

        return sink_fresh

    def sink_low(i, cols, product):
        proj[pl.ds(0, slots), cols] = product

    def home(j):
        norm_rows(hid.at[pl.ds(0, slots)], 2 * c + j, 0, 1, 0)
        first = normed.at[pl.ds(0, slots)]
        multiply(first, wbuf.at[1], sink_low)
        rms_rows(
            fresh_stage.at[j],
            slice(0, model),
            slice(model, 2 * model),
            1.0,
            0,
            slots,
            0,
            counts[j, z],
        )
        multiply(first, wbuf.at[2], sink_fresh_of(j))
        fresh_out(j).start()

    def first_parts():
        parts_first(1)
        parts_first(3)
        across_start(2)
        kv_start(0, 1)
        kv_start(1, 1)

    @pl.when(s == 0)
    def _():
        def enter(k, carry):
            for part in range(2):
                cols = pl.ds(part * half, half)
                remote(
                    lat_owner.at[k, :, cols],
                    lat_owner.at[k, :, cols],
                    lo_send.at[0],
                    lo_recv.at[k, part],
                    sibling,
                ).wait_recv()
            base = pl.multiple_of(k * slots, slots)
            embed_rows(lat_owner.at[k], base)
            norm_rows(hid.at[pl.ds(base, slots)], z, 0, 1, base)
            return carry

        values_ready()
        first_parts()
        lax.fori_loop(0, 2, enter, 0)
        weights_arrive(0)
        project(0, 0, 2 * slots)
        keys_early()
        parts_second(1)
        project(1, 0, 2 * slots)
        for k in range(2):
            mask_keys(2 * c + k, k_buf, k * slots)
        parts_second(3)
        caches_arrive()
        weights_arrive(2)

        def leave(turn, carry):
            k = lax.rem(turn + z, 2)
            base = pl.multiple_of(k * slots, slots)
            multiply(normed.at[pl.ds(base, slots)], wbuf.at[2], sink_value_of(k, base))
            attend(k, base)

            def after(i, cols, hidden):
                h1_stage[k, :, cols] = hidden.astype(jnp.bfloat16)
                h1_over(k, i).start()

            update(k, base, after)
            return carry

        lax.fori_loop(0, 2, leave, 0)

        def home_first(j, carry):
            for part in range(2):
                cols = pl.ds(part * half, half)
                remote(
                    lat_home.at[j, :, cols],
                    lat_home.at[j, :, cols],
                    lh_send.at[0],
                    lh_recv.at[j, part],
                    sibling,
                ).wait_recv()
            embed_rows(lat_home.at[j], 0)
            home(j)
            return carry

        kv_sent()
        lax.fori_loop(0, 2, home_first, 0)
        for k in range(2):
            for i in range(tiles):
                h1_over(k, i).wait_send()

    @pl.when(s == 1)
    def _():
        values_ready()
        first_parts()
        weights_arrive(0)
        keys_early()
        parts_second(1)
        parts_second(3)
        caches_arrive()
        weights_arrive(2)

        def turn_of(turn, carry):
            k = lax.rem(turn + z, 2)
            base = pl.multiple_of(k * slots, slots)
            rows = pl.ds(base, slots)

            @pl.when(turn == 0)
            def _():
                for i in range(tiles):
                    h1_arrives(k, i)

            @pl.when(turn == 1)
            def _():
                h1_arrives(k, tiles - 1)

            other = pl.multiple_of(slots - base, slots)
            here, there = normed.at[rows], normed.at[pl.ds(other, slots)]
            j = lax.rem(turn + z, 2)
            norm_rows(h1_buf.at[k], z, 0, 1, base)

            def sink_high(i, cols, product):
                proj[pl.ds(slots, slots), cols] = product

            def query_rows(at):
                rms_block(q_buf, slice(None), slice(0, model), factor, 0, at, base, None)

            last_row = meta[z, pl.ds(5 + 2 * c + k, 1), :]

            def key_rows(at):
                rms_block(
                    k_buf, slice(None), slice(model, 2 * model), 1.0, slots, at, base, None
                )
                first = k_buf[pl.ds(base, 16), :][0:1, :].astype(jnp.float32)
                row = lax.broadcasted_iota(jnp.int32, (16, model), 0) + at
                mine = pl.ds(base + at, 16)
                k_buf[mine, :] = jnp.where(
                    row.astype(jnp.float32) < last_row, k_buf[mine, :].astype(jnp.float32), first
                ).astype(jnp.bfloat16)

            def home_rows(at):
                norm_block(h1_home.at[j], 2 * c + j, 0, 1, other, at)

            def fresh_rows(at):
                rms_block(
                    fresh_stage.at[j],
                    slice(0, model),
                    slice(model, 2 * model),
                    1.0,
                    0,
                    at,
                    0,
                    counts[j, z],
                )

            def sink_update(i, cols, product):
                hid[rows, cols] = (
                    h1_buf[k, :, cols].astype(jnp.float32) + meta[z, 2:3, cols] * product
                )

            multiply_beside(here, wbuf.at[0], sink_low, None)
            multiply_beside(here, wbuf.at[1], sink_high, query_rows)
            multiply_beside(here, wbuf.at[2], sink_value_of(k, base), key_rows)

            @pl.when(turn == 0)
            def _():
                h1_arrives(1 - k, 0)

            attend(k, base)

            @pl.when(turn == 0)
            def _():
                h1_arrives(1 - k, 1)

            for i in range(tiles):
                remote(
                    h1_tile(h1_home.at[j], i),
                    h1_tile(h1_home.at[j], i),
                    hh_send.at[0, i],
                    hh_recv.at[j, i],
                    sibling,
                ).wait_recv()
            multiply_beside(attended, wbuf.at[3], sink_update, home_rows)
            norm_rows(hid.at[rows], z, 3, 4, base)
            vel_stage[k] = lax.dot_general(
                head_weight[...],
                normed[rows, :],
                (((1,), (1,)), ((), ())),
                preferred_element_type=jnp.float32,
            )
            vel_to_home(k, 0).start()

            @pl.when(home_is_self(k))
            def _():
                pltpu.make_async_copy(vel_src(k, 1), vel_buf.at[spot], vel_recv.at[spot]).start()

            @pl.when(jnp.logical_not(home_is_self(k)))
            def _():
                vel_to_home(k, 1).start()

            multiply_beside(there, wbuf.at[1], sink_low, None)
            multiply_beside(there, wbuf.at[2], sink_fresh_of(j), fresh_rows)
            fresh_out(j).start()
            return carry

        kv_sent()
        lax.fori_loop(0, 2, turn_of, 0)
        for k in range(2):
            vel_to_home(k, 0).wait_send()

            @pl.when(jnp.logical_not(home_is_self(k)))
            def _():
                for i in range(tiles):
                    h1_to_home(k, i).wait_send()
                vel_to_home(k, 1).wait_send()

    for t in range(4):
        for dg in range(1, chips):
            w_across(t, dg).wait_send()
            if t not in SHARED:
                w_forward(t, dg).wait_send()
        w_sibling(t).wait_send()
    parts_sent()
    for j in range(2):

        @pl.when(jnp.logical_not(lat_owner_self(j)))
        def _():
            lat_owner_copy(j).wait_send()

        @pl.when(s == 1)
        def _():
            lat_home_copy(j).wait_send()

    for j in range(2):
        remote(
            vel_buf.at[j], vel_buf.at[j], vel_send.at[0, 0], vel_recv.at[j], sibling
        ).wait_recv()
        slot = lax.broadcasted_iota(jnp.int32, vel_buf.shape[1:], 1) + s * half
        step = jnp.full(vel_buf.shape[1:], steps[j].astype(jnp.float32))
        value = jnp.where(slot < counts[j, z], vel_buf[j], 0.0)
        velocity[j, 0] = value
        new_latent[j, 0] = latent[j, 0] + (sigma_of(step + 1.0) - sigma_of(step)) * value
        fresh_out(j).wait()


def hand_on(velocity_in, latent_in, fresh_in, velocity, new_latent, fresh):
    velocity[...] = velocity_in[...]
    new_latent[...] = latent_in[...]
    fresh[...] = fresh_in[...]


def body(
    chips,
    latent,
    counts,
    steps_idx,
    embed_weight,
    wqkv,
    wo,
    qk_gain,
    modulation,
    head_mod,
    head_weight,
    stale_cache,
):
    videos, _, half, channels = latent.shape
    patches = counts.shape[1]
    slots = stale_cache.shape[3]
    model = embed_weight.shape[1]
    assert videos == 2 and patches == 4
    bf16, f32 = jnp.bfloat16, jnp.float32
    vmem = pl.BlockSpec(memory_space=pltpu.VMEM)
    smem = pl.BlockSpec(memory_space=pltpu.SMEM)
    anywhere = pl.BlockSpec(memory_space=pl.ANY)
    dma = pltpu.SemaphoreType.DMA
    latent = jnp.swapaxes(latent, 2, 3)
    velocity, new_latent, fresh = pl.pallas_call(
        functools.partial(step_kernel, chips),
        in_specs=[vmem, smem, smem, vmem] + [anywhere] * 7,
        out_specs=[vmem, vmem, anywhere],
        out_shape=[
            jax.ShapeDtypeStruct(latent.shape, f32),
            jax.ShapeDtypeStruct(latent.shape, f32),
            jax.ShapeDtypeStruct(stale_cache.shape, bf16),
        ],
        scratch_shapes=[
            pltpu.VMEM(embed_weight.shape, bf16),
            pltpu.VMEM((modulation.shape[1], 1, 3 * model), f32),
            pltpu.VMEM(head_mod.shape, f32),
            pltpu.VMEM((channels, model), bf16),
            dma((4,)),
            dma((2,)),
            pltpu.VMEM((4, model, model), bf16),
            pltpu.VMEM((2, patches, slots, model), bf16),
            pltpu.VMEM((patches, slots, HD), bf16),
            pltpu.VMEM((4, META_ROWS, model), f32),
            pltpu.VMEM((2, channels, half), bf16),
            pltpu.VMEM((2, channels, slots), bf16),
            pltpu.VMEM((2, channels, slots), bf16),
            pltpu.VMEM((2 * slots, model), f32),
            pltpu.VMEM((2 * slots, model), f32),
            pltpu.VMEM((2 * slots, model), bf16),
            pltpu.VMEM((2 * slots, model), bf16),
            pltpu.VMEM((2 * slots, model), bf16),
            pltpu.VMEM((2 * slots, model), bf16),
            pltpu.VMEM((slots, model), bf16),
            pltpu.VMEM((2, slots, model), bf16),
            pltpu.VMEM((2, slots, model), bf16),
            pltpu.VMEM((2, slots, model), bf16),
            pltpu.VMEM((2, slots, 2 * model), bf16),
            pltpu.VMEM((2, channels, slots), f32),
            pltpu.VMEM((2, channels, half), f32),
            dma((4,)),
            dma((4, chips)),
            dma((4, chips)),
            dma((4,)),
            dma((4,)),
            dma((3, chips)),
            dma((3, chips)),
            dma((2, chips)),
            dma((2, chips)),
            dma((2, chips, 2)),
            dma((2, chips, 2)),
            dma((2, 2)),
            dma((patches,)),
            dma((patches,)),
            dma((patches,)),
            dma,
            dma,
            dma((2,)),
            dma((2, 2)),
            dma((2,)),
            dma((2, 2)),
            dma((2, model // TILE)),
            dma((2, model // TILE)),
            dma((2, model // TILE)),
            dma((2, model // TILE)),
            dma((2, 2)),
            dma((2,)),
            dma((2,)),
        ],
        compiler_params=pltpu.CompilerParams(
            collective_id=0, has_side_effects=True, vmem_limit_bytes=58 * 1024 * 1024
        ),
    )(
        latent,
        counts,
        steps_idx,
        qk_gain,
        embed_weight,
        jnp.swapaxes(modulation, 0, 1),
        head_mod,
        head_weight.T,
        wqkv,
        wo,
        stale_cache,
    )
    small = pl.BlockSpec(velocity.shape, lambda i: (0, 0, 0, 0))
    large = pl.BlockSpec((1, 1, 1, slots, 2 * model), lambda i: (0, i, 0, 0, 0))
    velocity, new_latent, fresh = pl.pallas_call(
        hand_on,
        grid=(2,),
        in_specs=[small, small, large],
        out_specs=[small, small, large],
        out_shape=[jax.ShapeDtypeStruct(a.shape, a.dtype) for a in (velocity, new_latent, fresh)],
    )(velocity, new_latent, fresh)
    return jnp.swapaxes(velocity, 2, 3), jnp.swapaxes(new_latent, 2, 3), fresh


def solution(mesh):
    chips = mesh.shape["fsdp"] // 2
    in_specs = (
        P("fsdp", "patch", "section", None),
        P("fsdp", None),
        P("fsdp"),
        P(),
        P("section", "fsdp", None),
        P("section", "fsdp", None),
        P("section", None),
        P("section", None, None),
        P(),
        P(),
        P("section", "fsdp", "patch", None, None),
    )
    out_specs = (
        P("fsdp", "patch", "section", None),
        P("fsdp", "patch", "section", None),
        P("section", "fsdp", "patch", None, None),
    )
    return jax.shard_map(
        functools.partial(body, chips),
        mesh=mesh,
        in_specs=in_specs,
        out_specs=out_specs,
        check_vma=False,
    )
```
